512 devices in a mesh: dp: 64 (over y, z), tensor: 8 (over x, core).
Axes of the slice: x: 4, y: 8, z: 8, core: 2. Of those that a mesh axis runs over, the one named last changes fastest.
Arguments:
- activations: bfloat16 [81920, 5120], P('dp', 'tensor'), may hold values from -6 to 6
- cotangents: bfloat16 [81920, 1024], P('dp', 'tensor'), as said below
- error_old: bfloat16 [327680, 1024], P(('dp', 'tensor')), may hold values from -3 to 3
- pause_positions: int32 [320], replicated, may hold values from 0 to 1279, as said below
- initial_q: float32 [1024, 32], replicated, may hold values from -6 to 6
Outputs:
- error_new: bfloat16 [327680, 1024], P(('dp', 'tensor'))
- q_factor: float32 [1024, 32], P('tensor')
The draws below stay inside these ranges and needn't reach their ends.
Inputs may be any that keep to these rules, and one draw needn't show every extreme that they name: pause_positions holds 320 different padding positions of a replica's batch, which attention masks out, in no particular order; they are the same for every replica. cotangents lie within 6 / sqrt(1280) in magnitude.
All inputs are finite; a program needn't handle non-finite values.
Results may differ from the reference program's by a relative error of at most 0.002.
Values may be sent and summed in bfloat16 or wider, within the bound.
No kernel may reach another device: no remote copies, remote signals or barrier semaphores. Data moves between devices by JAX's collectives and lax.ppermute only.
A program may use at most 64 MiB of HBM per device.

```python
import jax
import jax.numpy as jnp
from jax import lax

D = 5120
KW = 1024
R = 32
TOK_REP = 1280
PAUSES = 320
TOKENS = 81920
N_DP = 64


def mixed_draw(key, row_count, col_count, mixing):
    replicas = TOKENS // TOK_REP
    common = jax.random.normal(jax.random.fold_in(key, 11), (row_count, col_count), jnp.float32)
    private = jax.random.normal(jax.random.fold_in(key, 12), (replicas * row_count, col_count), jnp.float32)
    whole = mixing ** 0.5 * jnp.tile(common, (replicas, 1)) + (1.0 - mixing) ** 0.5 * private
    return jnp.clip(whole, -6.0, 6.0)


def draw_activations(key, part):
    return mixed_draw(jax.random.fold_in(key, 101), TOK_REP, D, 0.8).astype(jnp.bfloat16)


def draw_cotangents(key, part):
    scaled = mixed_draw(jax.random.fold_in(key, 202), TOK_REP, KW, 0.8) * TOK_REP ** (-0.5)
    return scaled.astype(jnp.bfloat16)


def draw_pause_positions(key, part):
    shuffled = jax.random.permutation(jax.random.fold_in(key, 303), TOK_REP)
    return shuffled[:PAUSES].astype(jnp.int32)


def block_scale(own_key, extent, pieces, low, largest):
    level, own = 1.0, jax.random.fold_in(own_key, 6)
    for dim, parts in pieces:
        draws = jnp.exp(jax.random.uniform(jax.random.fold_in(own, dim), (parts,), jnp.float32, low / len(pieces), largest / len(pieces)))
        level = level * jnp.repeat(draws, extent[dim] // parts).reshape([-1 if axis == dim else 1 for axis in range(len(extent))])
    return level


def gaussian(key, dims, spread, most, shards=(), held_as=jnp.bfloat16):
    result = spread * jax.random.normal(key, dims, jnp.float32)
    if shards:
        result = result * block_scale(key, dims, shards, -0.22, 0.18)
    return jnp.clip(result, -most, most).astype(held_as)


def setup_inputs(seed: int = 0) -> dict:
    seeds = jax.random.split(jax.random.key(seed), 6)
    return {
        "activations": draw_activations(jax.random.fold_in(seeds[5], 71), 0),
        "cotangents": draw_cotangents(jax.random.fold_in(seeds[5], 71), 0),
        "error_old": gaussian(seeds[2], (N_DP * D, KW), 0.5, 3.0, ((0, 512),)),
        "pause_positions": draw_pause_positions(jax.random.fold_in(seeds[5], 71), 0),
        "initial_q": gaussian(seeds[4], (KW, R), 1.0, 6.0, (), jnp.float32),
    }


def kept_mask(pause_positions, row_count):
    positions = jnp.arange(row_count, dtype=jnp.int32)
    struck = jnp.any(positions[:, None] == pause_positions[None, :], axis=1)
    return jnp.where(struck, 0, 1).astype(jnp.int32)

def orthonormal(matrix):
    columns = []
    for position in range(matrix.shape[1]):
        column = matrix[:, position]
        for basis in columns:
            column = column - jnp.dot(basis, column, precision=lax.Precision.HIGHEST) * basis
        column = column / jnp.sqrt(jnp.sum(column * column))
        columns.append(column)
    return jnp.stack(columns, axis=1)

def reference(activations, cotangents, error_old, pause_positions, initial_q):
    weights = kept_mask(pause_positions, TOK_REP).astype(jnp.bfloat16)
    contract = (((0,), (0,)), ((), ()))

    def merged_of(replica):
        row_start = (replica * TOK_REP).astype(jnp.int32)
        err_start = (replica * D).astype(jnp.int32)
        feat_rows = lax.dynamic_slice_in_dim(activations, row_start, TOK_REP, 0)
        cot_rows = lax.dynamic_slice_in_dim(cotangents, row_start, TOK_REP, 0) * weights[:, None]
        gradient = lax.dot_general(feat_rows, cot_rows, contract, preferred_element_type=jnp.float32)
        return gradient + lax.dynamic_slice_in_dim(error_old, err_start, D, 0).astype(jnp.float32)

    def accumulate(replica, running):
        return running + merged_of(jnp.asarray(replica).astype(jnp.int32))
    summed = lax.fori_loop(0, N_DP, accumulate, jnp.zeros((D, KW), jnp.float32))
    mean_merged = summed / N_DP
    left_raw = jnp.dot(mean_merged, initial_q, precision=lax.Precision.HIGHEST)
    left_basis = orthonormal(left_raw)
    q_factor = jnp.dot(mean_merged.T, left_basis, precision=lax.Precision.HIGHEST)
    update = jnp.dot(left_basis, q_factor.T, precision=lax.Precision.HIGHEST)

    def fresh_error(replica):
        return (merged_of(replica) - update).astype(jnp.bfloat16)
    errors = lax.map(fresh_error, jnp.arange(N_DP, dtype=jnp.int32))
    return (errors.reshape(N_DP * D, KW), q_factor)
```

```python
import functools

import jax
import jax.numpy as jnp
from jax import lax
from jax.experimental import pallas as pl
from jax.experimental.pallas import tpu as pltpu
from jax.sharding import Mesh
from jax.sharding import PartitionSpec as P

DP = ("y", "z")
TENSOR = ("x", "c")
NEAR = ("z", "c")
FAR = ("y", "x")
CHUNK = 256
MIB = 1024 * 1024
F32 = jnp.float32
BF16 = jnp.bfloat16


def dot(a, b, contract, precision=None):
    return lax.dot_general(
        a, b, (contract, ((), ())), precision=precision, preferred_element_type=F32
    )


def params():
    return pltpu.CompilerParams(vmem_limit_bytes=24 * MIB)


def split(x):
    high = x.astype(BF16)
    return high, (x - high.astype(F32)).astype(BF16)


def selection(pauses, row_count, kept_count):
    count = pauses.shape[1]
    row = lax.broadcasted_iota(jnp.int32, (count, count), 0)
    col = lax.broadcasted_iota(jnp.int32, (count, count), 1)
    column = jnp.sum(
        jnp.where(row == col, pauses.astype(F32), 0.0), axis=1, keepdims=True
    )
    spot = lax.broadcasted_iota(jnp.int32, (1, row_count), 1).astype(F32)
    before = jnp.sum(jnp.where(column < spot, 1.0, 0.0), axis=0, keepdims=True)
    struck = jnp.sum(jnp.where(column == spot, 1.0, 0.0), axis=0, keepdims=True)
    target = jnp.where(struck > 0.0, -1.0, spot - before)
    rank = lax.broadcasted_iota(jnp.int32, (kept_count, row_count), 0).astype(F32)
    return jnp.where(rank == target, 1.0, 0.0).astype(BF16)


def compact_cotangents_kernel(pause_ref, cot_ref, out_ref):
    pick = selection(pause_ref[...], cot_ref.shape[0], out_ref.shape[1])
    kept = dot(pick, cot_ref[...], ((1,), (0,))).astype(BF16)
    for copy in range(out_ref.shape[0]):
        out_ref[copy] = kept


def compact_features_kernel(pause_ref, act_ref, out_ref, pick_ref):
    @pl.when(pl.program_id(0) == 0)
    def _():
        pick_ref[...] = selection(pause_ref[...], act_ref.shape[0], out_ref.shape[0])

    out_ref[...] = dot(pick_ref[...], act_ref[...], ((1,), (0,))).astype(BF16)


def merge_kernel(core_ref, feat_ref, own_ref, other_ref, err_ref, q_ref, merged_ref, left_ref, acc_ref):
    step = pl.program_id(0)
    first = core_ref[0] == 0
    own, other = own_ref[0], other_ref[0]
    low = jnp.where(first, own, other)
    high = jnp.where(first, other, own)
    cots = jnp.concatenate([low, high], axis=1)
    merged = dot(feat_ref[...], cots, ((0,), (0,))) + err_ref[...].astype(F32)
    merged_ref[...] = merged
    m_high, m_low = split(merged)
    q_high, q_low = split(q_ref[...])
    rank = q_high.shape[0]
    both = dot(jnp.concatenate([q_high, q_low], axis=0), m_high, ((1,), (1,)))
    part = both[:rank] + both[rank:] + dot(q_high, m_low, ((1,), (1,)))

    @pl.when(step == 0)
    def _():
        acc_ref[...] = part

    @pl.when(step > 0)
    def _():
        acc_ref[...] += part

    @pl.when(step == pl.num_programs(0) - 1)
    def _():
        total = acc_ref[...].astype(BF16)
        for copy in range(left_ref.shape[0]):
            left_ref[copy] = total


def add_copies_kernel(in_ref, out_ref):
    total = in_ref[0].astype(F32)
    for copy in range(1, in_ref.shape[0]):
        total += in_ref[copy].astype(F32)
    total = total.astype(out_ref.dtype)
    for copy in range(out_ref.shape[0]):
        out_ref[copy] = total


def project_kernel(replicas, in_ref, merged_ref, left_ref, out_ref, halves_ref):
    step = pl.program_id(0)
    last = pl.num_programs(0) - 1
    rank = left_ref.shape[0]

    @pl.when(step == 0)
    def _():
        total = in_ref[0].astype(F32)
        for copy in range(1, in_ref.shape[0]):
            total += in_ref[copy].astype(F32)
        total = total / replicas
        left_ref[...] = total
        high, low = split(total)
        halves_ref[:rank] = high
        halves_ref[rank:] = low

    @pl.when(step < last)
    def _():
        m_high, m_low = split(merged_ref[...])
        both = dot(halves_ref[...], m_high, ((1,), (0,)))
        part = both[:rank] + both[rank:] + dot(halves_ref[:rank], m_low, ((1,), (0,)))
        lines = out_ref.shape[1]
        for piece in range(out_ref.shape[0]):
            out_ref[piece] = part[piece * lines : (piece + 1) * lines]

    @pl.when(step == last)
    def _():
        left = left_ref[...]
        gram = dot(left, left, ((1,), (1,)), lax.Precision.HIGHEST)
        wide = jnp.concatenate([gram, jnp.zeros((rank, out_ref.shape[2] - rank), F32)], axis=1)
        lines = out_ref.shape[1]
        for piece in range(out_ref.shape[0]):
            out_ref[piece] = wide[piece * lines : (piece + 1) * lines]


def inverse_factor(gram):
    rank = gram.shape[0]
    row = lax.broadcasted_iota(jnp.int32, (rank, rank), 0)
    col = lax.broadcasted_iota(jnp.int32, (rank, rank), 1)
    table = jnp.concatenate([gram, jnp.where(row == col, 1.0, 0.0)], axis=1)
    line = lax.broadcasted_iota(jnp.int32, (rank, 1), 0)
    for k in range(rank):
        column = table[:, k : k + 1]
        pivot = table[k : k + 1, k : k + 1]
        weight = jnp.where(line > k, column / pivot, 0.0)
        table = table - weight * table[k : k + 1, :]
    diagonal = jnp.sum(jnp.where(row == col, table[:, :rank], 0.0), axis=1, keepdims=True)
    return table[:, rank:] / jnp.sqrt(diagonal)


def finish_kernel(replicas, place_ref, in_ref, left_ref, merged_ref, err_ref, own_ref, q_ref, lhs_ref, rhs_ref):
    step = pl.program_id(0)
    rank, width = q_ref.shape

    @pl.when(step == 0)
    def _():
        table = jnp.concatenate([in_ref[piece] for piece in range(in_ref.shape[0])], axis=0)
        table = table / replicas
        inverse = inverse_factor(table[:, width : width + rank])
        q_new = dot(inverse, table[:, :width], ((1,), (0,)), lax.Precision.HIGHEST)
        basis = dot(inverse, left_ref[...], ((1,), (0,)), lax.Precision.HIGHEST)
        q_ref[...] = q_new
        q_high, q_low = split(q_new)
        b_high, b_low = split(basis)
        lhs_ref[...] = jnp.concatenate([b_high, b_low, b_high], axis=0)
        rhs_ref[...] = jnp.concatenate([q_high, q_high, q_low], axis=0)
        lanes = own_ref.shape[1]
        start = pl.multiple_of(place_ref[0] * lanes, lanes)
        own_ref[...] = q_ref[:, pl.ds(start, lanes)]

    here = pl.multiple_of(step * CHUNK, CHUNK)
    update = dot(lhs_ref[...], rhs_ref[:, pl.ds(here, CHUNK)], ((0,), (0,)))
    err_ref[...] = (merged_ref[...] - update).astype(BF16)


def whole(shape):
    return pl.BlockSpec(shape, lambda *_: (0,) * len(shape))


def scalar():
    return pl.BlockSpec(memory_space=pltpu.SMEM)


def to_all(pieces, axes):
    return lax.all_to_all(pieces, axes, split_axis=0, concat_axis=0, tiled=True)


def add_copies(x, count, dtype):
    return pl.pallas_call(
        add_copies_kernel,
        out_shape=jax.ShapeDtypeStruct((count, *x.shape[1:]), dtype),
        compiler_params=params(),
        name="add_copies",
    )(x)


def body(activations, cotangents, error_old, pause_positions, initial_q):
    row_count, features = activations.shape
    lanes = cotangents.shape[1]
    width, rank = initial_q.shape
    kept_count = row_count - pause_positions.shape[0]
    replicas = lax.axis_size(DP)
    line_x, across = lax.axis_size("x"), lax.axis_size("z")
    near, far = lax.axis_size(NEAR), lax.axis_size(FAR)
    chunks = width // CHUNK
    core = lax.axis_index("c").astype(jnp.int32).reshape(1)
    place = lax.axis_index(TENSOR).astype(jnp.int32).reshape(1)
    pauses = pause_positions.reshape(1, -1)

    cot_copies = pl.pallas_call(
        compact_cotangents_kernel,
        out_shape=jax.ShapeDtypeStruct((line_x, kept_count, lanes), BF16),
        compiler_params=params(),
        name="compact_cotangents",
    )(pauses, cotangents)
    own = to_all(cot_copies, "x")
    halves = 5 if features % 640 == 0 else 1
    kept_features = pl.pallas_call(
        compact_features_kernel,
        grid=(halves,),
        in_specs=[
            whole(pauses.shape),
            pl.BlockSpec((row_count, features // halves), lambda i: (0, i)),
        ],
        out_specs=pl.BlockSpec((kept_count, features // halves), lambda i: (0, i)),
        out_shape=jax.ShapeDtypeStruct((kept_count, features), BF16),
        scratch_shapes=[pltpu.VMEM((kept_count, row_count), BF16)],
        compiler_params=params(),
        cost_estimate=pl.CostEstimate(
            flops=2 * kept_count * row_count * features,
            bytes_accessed=4 * row_count * features,
            transcendentals=0,
        ),
        name="compact_features",
    )(pauses, activations)
    cores = lax.axis_size("c")
    other = lax.ppermute(own, "c", [(i, cores - 1 - i) for i in range(cores)])

    merged, left_copies = pl.pallas_call(
        merge_kernel,
        grid=(chunks,),
        in_specs=[
            scalar(),
            whole((kept_count, features)),
            pl.BlockSpec((1, kept_count, lanes), lambda i: (i, 0, 0)),
            pl.BlockSpec((1, kept_count, lanes), lambda i: (i, 0, 0)),
            pl.BlockSpec((features, CHUNK), lambda i: (0, i)),
            pl.BlockSpec((rank, CHUNK), lambda i: (0, i)),
        ],
        out_specs=[
            pl.BlockSpec((features, CHUNK), lambda i: (0, i)),
            whole((across, rank, features)),
        ],
        out_shape=[
            jax.ShapeDtypeStruct((features, width), F32),
            jax.ShapeDtypeStruct((across, rank, features), BF16),
        ],
        scratch_shapes=[pltpu.VMEM((rank, features), F32)],
        compiler_params=params(),
        name="merge",
    )(core, kept_features, own, other, error_old, initial_q.T)

    left_copies = add_copies(to_all(left_copies, "z"), lax.axis_size("y"), BF16)
    left_copies = to_all(left_copies, "y")

    left, q_pieces = pl.pallas_call(
        functools.partial(project_kernel, replicas),
        grid=(chunks + 1,),
        in_specs=[
            whole(left_copies.shape),
            pl.BlockSpec((features, CHUNK), lambda i: (0, jnp.minimum(i, chunks - 1))),
        ],
        out_specs=[
            whole((rank, features)),
            pl.BlockSpec((near, rank // near, CHUNK), lambda i: (0, 0, i)),
        ],
        out_shape=[
            jax.ShapeDtypeStruct((rank, features), F32),
            jax.ShapeDtypeStruct((near, rank // near, width + CHUNK), F32),
        ],
        scratch_shapes=[pltpu.VMEM((2 * rank, features), BF16)],
        compiler_params=params(),
        name="project",
    )(left_copies, merged)

    q_pieces = add_copies(to_all(q_pieces, NEAR), far, F32)
    q_pieces = add_copies(to_all(q_pieces, FAR), near, F32)
    q_pieces = to_all(q_pieces, NEAR)

    error_new, own_q = pl.pallas_call(
        functools.partial(finish_kernel, replicas),
        grid=(chunks,),
        in_specs=[
            scalar(),
            whole(q_pieces.shape),
            whole((rank, features)),
            pl.BlockSpec((features, CHUNK), lambda i: (0, i)),
        ],
        out_specs=[
            pl.BlockSpec((features, CHUNK), lambda i: (0, i)),
            whole((rank, lanes)),
        ],
        out_shape=[
            jax.ShapeDtypeStruct((features, width), BF16),
            jax.ShapeDtypeStruct((rank, lanes), F32),
        ],
        scratch_shapes=[
            pltpu.VMEM((rank, width), F32),
            pltpu.VMEM((3 * rank, features), BF16),
            pltpu.VMEM((3 * rank, width), BF16),
        ],
        compiler_params=params(),
        name="finish",
    )(place, q_pieces, left, merged)
    return error_new, own_q.T


def solution(mesh, sizes=(8, 8, 4, 2)):
    finer = Mesh(mesh.devices.reshape(sizes), ("y", "z", "x", "c"))
    everyone = ("y", "z", "x", "c")
    in_specs = (P(DP, TENSOR), P(DP, TENSOR), P(everyone, None), P(), P())
    out_specs = (P(everyone, None), P(TENSOR, None))
    return jax.shard_map(
        body, mesh=finer, in_specs=in_specs, out_specs=out_specs, check_vma=False
    )
```

```python
import functools

import jax
import jax.numpy as jnp
from jax import lax
from jax.experimental import pallas as pl
from jax.experimental.pallas import tpu as pltpu
from jax.sharding import Mesh
from jax.sharding import PartitionSpec as P

DP = ("y", "z")
TENSOR = ("x", "c")
CHUNK = 256
LANES = 128
MIB = 1024 * 1024
F32 = jnp.float32
BF16 = jnp.bfloat16


def dot(a, b, contract, precision=None):
    return lax.dot_general(
        a, b, (contract, ((), ())), precision=precision, preferred_element_type=F32
    )


def params(limit=20 * MIB):
    return pltpu.CompilerParams(vmem_limit_bytes=limit)


def split(x):
    high = x.astype(BF16)
    return high, (x - high.astype(F32)).astype(BF16)


def selection(pauses, row_count, kept_count):
    count = pauses.shape[1]
    row = lax.broadcasted_iota(jnp.int32, (count, count), 0)
    col = lax.broadcasted_iota(jnp.int32, (count, count), 1)
    column = jnp.sum(
        jnp.where(row == col, pauses.astype(F32), 0.0), axis=1, keepdims=True
    )
    spot = lax.broadcasted_iota(jnp.int32, (1, row_count), 1).astype(F32)
    before = jnp.sum(jnp.where(column < spot, 1.0, 0.0), axis=0, keepdims=True)
    struck = jnp.sum(jnp.where(column == spot, 1.0, 0.0), axis=0, keepdims=True)
    target = jnp.where(struck > 0.0, -1.0, spot - before)
    rank = lax.broadcasted_iota(jnp.int32, (kept_count, row_count), 0).astype(F32)
    return jnp.where(rank == target, 1.0, 0.0).astype(BF16)


def compact_cotangents_kernel(pause_ref, cot_ref, out_ref):
    pick = selection(pause_ref[...], cot_ref.shape[0], out_ref.shape[1])
    kept = dot(pick, cot_ref[...], ((1,), (0,))).astype(BF16)
    for copy in range(out_ref.shape[0]):
        out_ref[copy] = kept


def compact_features_kernel(kept_count, pause_ref, act_ref, out_ref):
    pick = selection(pause_ref[...], act_ref.shape[0], kept_count)
    kept = dot(pick, act_ref[...], ((1,), (0,)))
    spare = jnp.zeros((out_ref.shape[1] - kept_count, kept.shape[1]), F32)
    out_ref[...] = jnp.concatenate([kept, spare], axis=0).T.astype(BF16)


def merge_kernel(feat_ref, own_ref, other_ref, err_ref, q_ref, merged_ref, left_ref):
    first = lax.axis_index("c") == 0
    pieces, kept_count, lanes = own_ref.shape
    rank = q_ref.shape[0]
    features, padded_count = feat_ref.shape
    q_high, q_low = split(q_ref[...])
    total = jnp.zeros((features, LANES), F32)
    for piece in range(pieces):
        own, other = own_ref[piece], other_ref[piece]
        cots = jnp.concatenate([jnp.where(first, own, other), jnp.where(first, other, own)], axis=1)
        cots = jnp.concatenate([cots, jnp.zeros((padded_count - kept_count, CHUNK), BF16)], axis=0)
        here = slice(piece * CHUNK, (piece + 1) * CHUNK)
        merged = dot(feat_ref[...], cots, ((1,), (0,))) + err_ref[:, here].astype(F32)
        merged_ref[:, here] = merged
        m_high, m_low = split(merged)
        high, low = q_high[:, here], q_low[:, here]
        upper = jnp.concatenate([high, high], axis=1)
        lower = jnp.concatenate([low, jnp.zeros_like(low)], axis=1)
        spare = jnp.zeros((LANES - 2 * rank, 2 * CHUNK), BF16)
        total += dot(
            jnp.concatenate([m_high, m_low], axis=1),
            jnp.concatenate([upper, lower, spare], axis=0),
            ((1,), (1,)),
        )
    turned = total.T
    left = (turned[:rank] + turned[rank : 2 * rank]).astype(BF16)
    for copy in range(left_ref.shape[0]):
        left_ref[copy] = left


def add_copies_kernel(in_ref, out_ref):
    total = in_ref[0].astype(F32)
    for copy in range(1, in_ref.shape[0]):
        total += in_ref[copy].astype(F32)
    total = total.astype(out_ref.dtype)
    for copy in range(out_ref.shape[0]):
        out_ref[copy] = total


def pack(gram, lines):
    rank = gram.shape[0]
    wide = jnp.concatenate([gram, jnp.zeros((rank, LANES - rank), F32)], axis=1)
    total = wide[:lines]
    for block in range(1, rank // lines):
        total += pltpu.roll(wide[block * lines : (block + 1) * lines], block * rank, 1)
    return total


def unpack(packed, rank):
    lines = packed.shape[0]
    blocks = [packed[:, :rank]]
    for block in range(1, rank // lines):
        blocks.append(pltpu.roll(packed, LANES - block * rank, 1)[:, :rank])
    return jnp.concatenate(blocks, axis=0)


def project_kernel(replicas, in_ref, merged_ref, left_ref, out_ref):
    rank = left_ref.shape[0]
    pieces, lines, lanes = out_ref.shape
    wide = CHUNK // lanes
    total = in_ref[0].astype(F32)
    for copy in range(1, in_ref.shape[0]):
        total += in_ref[copy].astype(F32)
    total = total / replicas
    left_ref[...] = total
    high, low = split(total)
    stack = jnp.concatenate([high, low], axis=0)
    gram = dot(total, total, ((1,), (1,)), lax.Precision.HIGHEST)
    packed = pack(gram, lines - rank)
    for chunk in range(pieces // wide):
        m_high, m_low = split(merged_ref[:, chunk * CHUNK : (chunk + 1) * CHUNK])
        both = dot(stack, m_high, ((1,), (0,)))
        part = both[:rank] + both[rank:] + dot(high, m_low, ((1,), (0,)))
        for piece in range(wide):
            here = chunk * wide + piece
            out_ref[here, :rank] = part[:, piece * lanes : (piece + 1) * lanes]
            out_ref[here, rank:] = packed


def add_blocks_kernel(rank, in_ref, out_ref, gram_ref):
    total = in_ref[0]
    for copy in range(1, in_ref.shape[0]):
        total += in_ref[copy]
    for copy in range(out_ref.shape[0]):
        out_ref[copy] = total[:rank]
    gram_ref[...] = total[rank:]


def inverse_factor(gram):
    rank = gram.shape[0]
    row = lax.broadcasted_iota(jnp.int32, (rank, rank), 0)
    col = lax.broadcasted_iota(jnp.int32, (rank, rank), 1)
    table = jnp.concatenate([gram, jnp.where(row == col, 1.0, 0.0)], axis=1)
    line = lax.broadcasted_iota(jnp.int32, (rank, 1), 0)
    for k in range(0, rank, 2):
        column, second = table[:, k : k + 1], table[:, k + 1 : k + 2]
        inverse = 1.0 / column[k : k + 1]
        slope = column[k + 1 : k + 2] * inverse
        pivot = second[k + 1 : k + 2] - slope * second[k : k + 1]
        top = table[k : k + 1, :]
        bottom = table[k + 1 : k + 2, :] - slope * top
        below = line > k + 1
        upper = jnp.where(below, column * inverse, 0.0)
        lower = jnp.where(below, (second - slope * column) / pivot, 0.0)
        table = jnp.where(line == k + 1, bottom, table - upper * top - lower * bottom)
    diagonal = jnp.sum(jnp.where(row == col, table[:, :rank], 0.0), axis=1, keepdims=True)
    return table[:, rank:] / jnp.sqrt(diagonal)


def finish_kernel(replicas, in_ref, gram_ref, left_ref, merged_ref, err_hbm, own_ref, q_ref, err_ref, sems):
    rank, width = q_ref.shape
    inverse = inverse_factor(unpack(gram_ref[...], rank))
    raw = jnp.concatenate([in_ref[piece] for piece in range(in_ref.shape[0])], axis=1)
    q_new = dot(inverse, raw / replicas, ((1,), (0,)), lax.Precision.HIGHEST)
    basis = dot(inverse, left_ref[...], ((1,), (0,)), lax.Precision.HIGHEST)
    q_ref[...] = q_new
    lanes = own_ref.shape[1]
    place = lax.axis_index("x") * lax.axis_size("c") + lax.axis_index("c")
    own_ref[...] = q_ref[:, pl.ds(pl.multiple_of(place * lanes, lanes), lanes)]
    high, low = split(q_new)
    stack = jnp.concatenate([high, high, low, jnp.zeros_like(high)], axis=0)
    high, low = split(basis)
    high = high.astype(F32)
    low = low.astype(F32)
    turned = jnp.concatenate([high, low, high, jnp.zeros_like(high)], axis=0).T.astype(BF16)
    stores = []
    chunks, rows, _ = err_ref.shape
    for chunk in range(chunks):
        here = slice(chunk * rows, (chunk + 1) * rows)
        update = dot(turned[here], stack, ((1,), (0,)))
        err_ref[chunk] = (merged_ref[here] - update).astype(BF16)
        stores.append(
            pltpu.make_async_copy(
                err_ref.at[chunk], err_hbm.at[pl.ds(chunk * rows, rows)], sems.at[chunk]
            )
        )
        stores[-1].start()
    for store in stores:
        store.wait()


def in_hbm():
    return pl.BlockSpec(memory_space=pltpu.HBM)


def whole(shape):
    return pl.BlockSpec(shape, lambda *_: (0,) * len(shape))


def to_all(pieces, axes):
    return lax.all_to_all(pieces, axes, split_axis=0, concat_axis=0, tiled=True)


def add_copies(x, count, dtype):
    return pl.pallas_call(
        add_copies_kernel,
        out_shape=jax.ShapeDtypeStruct((count, *x.shape[1:]), dtype),
        compiler_params=params(),
        name="add_copies",
    )(x)


def body(activations, cotangents, error_old, pause_positions, initial_q):
    row_count, features = activations.shape
    lanes = cotangents.shape[1]
    width, rank = initial_q.shape
    kept_count = row_count - pause_positions.shape[0]
    padded_count = -(-kept_count // CHUNK) * CHUNK
    replicas = lax.axis_size(DP)
    line_x, across = lax.axis_size("x"), lax.axis_size("z")
    crowd = lax.axis_size(TENSOR)
    chunks = width // CHUNK
    lines = rank * rank // LANES
    pauses = pause_positions.reshape(1, -1)

    cot_copies = pl.pallas_call(
        compact_cotangents_kernel,
        out_shape=jax.ShapeDtypeStruct((line_x, kept_count, lanes), BF16),
        compiler_params=params(),
        name="compact_cotangents",
    )(pauses, cotangents)
    own = to_all(cot_copies, "x")
    kept_features = pl.pallas_call(
        functools.partial(compact_features_kernel, kept_count),
        out_shape=jax.ShapeDtypeStruct((features, padded_count), BF16),
        compiler_params=params(),
        cost_estimate=pl.CostEstimate(
            flops=2 * kept_count * row_count * features,
            bytes_accessed=4 * row_count * features,
            transcendentals=0,
        ),
        name="compact_features",
    )(pauses, activations)
    cores = lax.axis_size("c")
    other = lax.ppermute(own, "c", [(i, cores - 1 - i) for i in range(cores)])

    merged, left_copies = pl.pallas_call(
        merge_kernel,
        out_shape=[
            jax.ShapeDtypeStruct((features, width), F32),
            jax.ShapeDtypeStruct((across, rank, features), BF16),
        ],
        compiler_params=params(),
        name="merge",
    )(kept_features, own, other, error_old, initial_q.T)

    left_copies = add_copies(to_all(left_copies, "z"), lax.axis_size("y"), BF16)
    left_copies = to_all(left_copies, "y")

    left, q_pieces = pl.pallas_call(
        functools.partial(project_kernel, replicas),
        out_shape=[
            jax.ShapeDtypeStruct((rank, features), F32),
            jax.ShapeDtypeStruct((crowd, rank + lines, lanes), F32),
        ],
        compiler_params=params(),
        name="project",
    )(left_copies, merged)

    q_copies, gram = pl.pallas_call(
        functools.partial(add_blocks_kernel, rank),
        out_shape=[
            jax.ShapeDtypeStruct((across, rank, lanes), F32),
            jax.ShapeDtypeStruct((lines, lanes), F32),
        ],
        compiler_params=params(),
        name="add_blocks",
    )(to_all(q_pieces, TENSOR))
    q_copies = add_copies(to_all(q_copies, "z"), lax.axis_size("y"), F32)
    q_copies = add_copies(to_all(q_copies, "y"), crowd, F32)
    q_pieces = to_all(q_copies, TENSOR)

    rows = features // 4
    error_new, own_q = pl.pallas_call(
        functools.partial(finish_kernel, replicas),
        out_specs=[in_hbm(), whole((rank, lanes))],
        out_shape=[
            jax.ShapeDtypeStruct((features, width), BF16),
            jax.ShapeDtypeStruct((rank, lanes), F32),
        ],
        scratch_shapes=[
            pltpu.VMEM((rank, width), F32),
            pltpu.VMEM((4, rows, width), BF16),
            pltpu.SemaphoreType.DMA((4,)),
        ],
        compiler_params=params(),
        name="finish",
    )(q_pieces, gram, left, merged)
    return error_new, own_q.T


def solution(mesh, sizes=(8, 8, 4, 2)):
    finer = Mesh(mesh.devices.reshape(sizes), ("y", "z", "x", "c"))
    everyone = ("y", "z", "x", "c")
    in_specs = (P(DP, TENSOR), P(DP, TENSOR), P(everyone, None), P(), P())
    out_specs = (P(everyone, None), P(TENSOR, None))
    return jax.shard_map(
        body, mesh=finer, in_specs=in_specs, out_specs=out_specs, check_vma=False
    )
```

```python
import functools

import jax
import jax.numpy as jnp
from jax import lax
from jax.experimental import pallas as pl
from jax.experimental.pallas import tpu as pltpu
from jax.sharding import Mesh
from jax.sharding import PartitionSpec as P

DP = ("y", "z")
TENSOR = ("x", "c")
CHUNK = 256
LANES = 128
BLOCKS = 5
MIB = 1024 * 1024
F32 = jnp.float32
BF16 = jnp.bfloat16


def dot(a, b, contract, precision=None):
    return lax.dot_general(
        a, b, (contract, ((), ())), precision=precision, preferred_element_type=F32
    )


def params(limit=20 * MIB):
    return pltpu.CompilerParams(vmem_limit_bytes=limit)


def split(x):
    high = x.astype(BF16)
    return high, (x - high.astype(F32)).astype(BF16)


def kept_ranks(pauses, row_count):
    count = pauses.shape[0]
    row = lax.broadcasted_iota(jnp.int32, (count, count), 0)
    col = lax.broadcasted_iota(jnp.int32, (count, count), 1)
    wide = pauses.astype(F32).reshape(1, count)
    column = jnp.sum(jnp.where(row == col, wide, 0.0), axis=1, keepdims=True)
    spot = lax.broadcasted_iota(jnp.int32, (1, row_count), 1).astype(F32)
    before = jnp.sum(jnp.where(column < spot, 1.0, 0.0), axis=0, keepdims=True)
    struck = jnp.sum(jnp.where(column == spot, 1.0, 0.0), axis=0, keepdims=True)
    return jnp.where(struck > 0.0, -1.0, spot - before)


def kept_rows(pauses, values_ref, kept_count):
    row_count = values_ref.shape[0]
    ranks = kept_ranks(pauses, row_count)
    size = kept_count // BLOCKS
    window = size + row_count - kept_count
    blocks = []
    for block in range(BLOCKS):
        start = block * size
        here = ranks if start == 0 else pltpu.roll(ranks, row_count - start, 1)
        rank = lax.broadcasted_iota(jnp.int32, (size, window), 0) + start
        pick = jnp.where(rank.astype(F32) == here[:, :window], 1.0, 0.0).astype(BF16)
        blocks.append(dot(pick, values_ref[start : start + window], ((1,), (0,))))
    return jnp.concatenate(blocks, axis=0)


def compact_cotangents_kernel(pause_ref, cot_ref, out_ref):
    kept = kept_rows(pause_ref[...], cot_ref, out_ref.shape[1]).astype(BF16)
    for copy in range(out_ref.shape[0]):
        out_ref[copy] = kept


def compact_features_kernel(kept_count, pause_ref, act_ref, out_ref):
    kept = kept_rows(pause_ref[...], act_ref, kept_count)
    spare = jnp.zeros((out_ref.shape[1] - kept_count, kept.shape[1]), F32)
    out_ref[...] = jnp.concatenate([kept, spare], axis=0).T.astype(BF16)


def merge_kernel(feat_ref, own_ref, other_ref, err_ref, q_ref, merged_ref, left_ref):
    first = lax.axis_index("c") == 0
    pieces, kept_count, lanes = own_ref.shape
    rank = q_ref.shape[0]
    features, padded_count = feat_ref.shape
    q_high, q_low = split(q_ref[...])
    total = jnp.zeros((features, LANES), F32)
    for piece in range(pieces):
        own, other = own_ref[piece], other_ref[piece]
        cots = jnp.concatenate([jnp.where(first, own, other), jnp.where(first, other, own)], axis=1)
        cots = jnp.concatenate([cots, jnp.zeros((padded_count - kept_count, CHUNK), BF16)], axis=0)
        here = slice(piece * CHUNK, (piece + 1) * CHUNK)
        merged = dot(feat_ref[...], cots, ((1,), (0,))) + err_ref[:, here].astype(F32)
        merged_ref[:, here] = merged
        m_high, m_low = split(merged)
        high, low = q_high[:, here], q_low[:, here]
        upper = jnp.concatenate([high, high], axis=1)
        lower = jnp.concatenate([low, jnp.zeros_like(low)], axis=1)
        spare = jnp.zeros((LANES - 2 * rank, 2 * CHUNK), BF16)
        total += dot(
            jnp.concatenate([m_high, m_low], axis=1),
            jnp.concatenate([upper, lower, spare], axis=0),
            ((1,), (1,)),
        )
    turned = total.T
    left = (turned[:rank] + turned[rank : 2 * rank]).astype(BF16)
    for copy in range(left_ref.shape[0]):
        left_ref[copy] = left


def add_copies_kernel(in_ref, out_ref):
    total = in_ref[0].astype(F32)
    for copy in range(1, in_ref.shape[0]):
        total += in_ref[copy].astype(F32)
    total = total.astype(out_ref.dtype)
    for copy in range(out_ref.shape[0]):
        out_ref[copy] = total


def pack(gram, lines):
    rank = gram.shape[0]
    wide = jnp.concatenate([gram, jnp.zeros((rank, LANES - rank), F32)], axis=1)
    total = wide[:lines]
    for block in range(1, rank // lines):
        total += pltpu.roll(wide[block * lines : (block + 1) * lines], block * rank, 1)
    return total


def unpack(packed, rank):
    lines = packed.shape[0]
    blocks = [packed[:, :rank]]
    for block in range(1, rank // lines):
        blocks.append(pltpu.roll(packed, LANES - block * rank, 1)[:, :rank])
    return jnp.concatenate(blocks, axis=0)


def project_kernel(replicas, in_ref, merged_ref, left_ref, out_ref):
    rank = left_ref.shape[0]
    pieces, lines, lanes = out_ref.shape
    wide = CHUNK // lanes
    total = in_ref[0].astype(F32)
    for copy in range(1, in_ref.shape[0]):
        total += in_ref[copy].astype(F32)
    total = total / replicas
    left_ref[...] = total
    high, low = split(total)
    stack = jnp.concatenate([high, low], axis=0)
    gram = dot(total, total, ((1,), (1,)), lax.Precision.HIGHEST)
    packed = pack(gram, lines - rank)
    for chunk in range(pieces // wide):
        m_high, m_low = split(merged_ref[:, chunk * CHUNK : (chunk + 1) * CHUNK])
        both = dot(stack, m_high, ((1,), (0,)))
        part = both[:rank] + both[rank:] + dot(high, m_low, ((1,), (0,)))
        for piece in range(wide):
            here = chunk * wide + piece
            out_ref[here, :rank] = part[:, piece * lanes : (piece + 1) * lanes]
            out_ref[here, rank:] = packed


def add_blocks_kernel(rank, in_ref, out_ref, gram_ref):
    total = in_ref[0]
    for copy in range(1, in_ref.shape[0]):
        total += in_ref[copy]
    for copy in range(out_ref.shape[0]):
        out_ref[copy] = total[:rank].astype(out_ref.dtype)
    gram_ref[...] = total[rank:]


def inverse_factor(gram):
    rank = gram.shape[0]
    row = lax.broadcasted_iota(jnp.int32, (rank, rank), 0)
    col = lax.broadcasted_iota(jnp.int32, (rank, rank), 1)
    table = jnp.concatenate([gram, jnp.where(row == col, 1.0, 0.0)], axis=1)
    line = lax.broadcasted_iota(jnp.int32, (rank, 1), 0)
    for k in range(0, rank, 2):
        column, second = table[:, k : k + 1], table[:, k + 1 : k + 2]
        inverse = 1.0 / column[k : k + 1]
        slope = column[k + 1 : k + 2] * inverse
        pivot = second[k + 1 : k + 2] - slope * second[k : k + 1]
        top = table[k : k + 1, :]
        bottom = table[k + 1 : k + 2, :] - slope * top
        below = line > k + 1
        upper = jnp.where(below, column * inverse, 0.0)
        lower = jnp.where(below, (second - slope * column) / pivot, 0.0)
        table = jnp.where(line == k + 1, bottom, table - upper * top - lower * bottom)
    diagonal = jnp.sum(jnp.where(row == col, table[:, :rank], 0.0), axis=1, keepdims=True)
    return table[:, rank:] / jnp.sqrt(diagonal)


def finish_kernel(replicas, in_ref, gram_ref, left_ref, merged_ref, err_hbm, own_ref, q_ref, err_ref, sems):
    rank, width = q_ref.shape
    inverse = inverse_factor(unpack(gram_ref[...], rank))
    raw = jnp.concatenate([in_ref[piece] for piece in range(in_ref.shape[0])], axis=1)
    raw = raw / replicas
    q_ref[...] = raw
    lanes = own_ref.shape[1]
    place = lax.axis_index("x") * lax.axis_size("c") + lax.axis_index("c")
    own = q_ref[:, pl.ds(pl.multiple_of(place * lanes, lanes), lanes)]
    own_ref[...] = dot(inverse, own, ((1,), (0,)), lax.Precision.HIGHEST)
    square = dot(inverse.T, inverse, ((1,), (0,)), lax.Precision.HIGHEST)
    high, low = split(dot(square, raw, ((1,), (0,)), lax.Precision.HIGHEST))
    stack = jnp.concatenate([high, high, low, jnp.zeros_like(high)], axis=0)
    high, low = split(left_ref[...])
    high = high.astype(F32)
    low = low.astype(F32)
    turned = jnp.concatenate([high, low, high, jnp.zeros_like(high)], axis=0).T.astype(BF16)
    stores = []
    chunks, rows, _ = err_ref.shape
    for chunk in range(chunks):
        here = slice(chunk * rows, (chunk + 1) * rows)
        update = dot(turned[here], stack, ((1,), (0,)))
        err_ref[chunk] = (merged_ref[here] - update).astype(BF16)
        stores.append(
            pltpu.make_async_copy(
                err_ref.at[chunk], err_hbm.at[pl.ds(chunk * rows, rows)], sems.at[chunk]
            )
        )
        stores[-1].start()
    for store in stores:
        store.wait()


def in_hbm():
    return pl.BlockSpec(memory_space=pltpu.HBM)


def whole(shape):
    return pl.BlockSpec(shape, lambda *_: (0,) * len(shape))


def to_all(pieces, axes):
    return lax.all_to_all(pieces, axes, split_axis=0, concat_axis=0, tiled=True)


def add_copies(x, count, dtype):
    return pl.pallas_call(
        add_copies_kernel,
        out_shape=jax.ShapeDtypeStruct((count, *x.shape[1:]), dtype),
        compiler_params=params(),
        name="add_copies",
    )(x)


def body(activations, cotangents, error_old, pause_positions, initial_q):
    row_count, features = activations.shape
    lanes = cotangents.shape[1]
    width, rank = initial_q.shape
    kept_count = row_count - pause_positions.shape[0]
    padded_count = -(-kept_count // CHUNK) * CHUNK
    replicas = lax.axis_size(DP)
    line_x, across = lax.axis_size("x"), lax.axis_size("z")
    crowd = lax.axis_size(TENSOR)
    chunks = width // CHUNK
    lines = rank * rank // LANES
    pauses = pause_positions

    cot_copies = pl.pallas_call(
        compact_cotangents_kernel,
        out_shape=jax.ShapeDtypeStruct((line_x, kept_count, lanes), BF16),
        compiler_params=params(),
        name="compact_cotangents",
    )(pauses, cotangents)
    own = to_all(cot_copies, "x")
    kept_features = pl.pallas_call(
        functools.partial(compact_features_kernel, kept_count),
        out_shape=jax.ShapeDtypeStruct((features, padded_count), BF16),
        compiler_params=params(),
        cost_estimate=pl.CostEstimate(
            flops=2 * kept_count * row_count * features,
            bytes_accessed=4 * row_count * features,
            transcendentals=0,
        ),
        name="compact_features",
    )(pauses, activations)
    cores = lax.axis_size("c")
    other = lax.ppermute(own, "c", [(i, cores - 1 - i) for i in range(cores)])

    merged, left_copies = pl.pallas_call(
        merge_kernel,
        out_shape=[
            jax.ShapeDtypeStruct((features, width), F32),
            jax.ShapeDtypeStruct((across, rank, features), BF16),
        ],
        compiler_params=params(),
        name="merge",
    )(kept_features, own, other, error_old, initial_q.T)

    left_copies = add_copies(to_all(left_copies, "z"), lax.axis_size("y"), BF16)
    left_copies = to_all(left_copies, "y")

    left, q_pieces = pl.pallas_call(
        functools.partial(project_kernel, replicas),
        out_shape=[
            jax.ShapeDtypeStruct((rank, features), F32),
            jax.ShapeDtypeStruct((crowd, rank + lines, lanes), F32),
        ],
        compiler_params=params(),
        name="project",
    )(left_copies, merged)

    q_copies, gram = pl.pallas_call(
        functools.partial(add_blocks_kernel, rank),
        out_shape=[
            jax.ShapeDtypeStruct((across, rank, lanes), BF16),
            jax.ShapeDtypeStruct((lines, lanes), F32),
        ],
        compiler_params=params(),
        name="add_blocks",
    )(to_all(q_pieces, TENSOR))
    q_copies = add_copies(to_all(q_copies, "z"), lax.axis_size("y"), F32)
    q_copies = add_copies(to_all(q_copies, "y"), crowd, F32)
    q_pieces = to_all(q_copies, TENSOR)

    parts = features // LANES
    error_new, own_q = pl.pallas_call(
        functools.partial(finish_kernel, replicas),
        out_specs=[in_hbm(), whole((rank, lanes))],
        out_shape=[
            jax.ShapeDtypeStruct((features, width), BF16),
            jax.ShapeDtypeStruct((rank, lanes), F32),
        ],
        scratch_shapes=[
            pltpu.VMEM((rank, width), F32),
            pltpu.VMEM((parts, LANES, width), BF16),
            pltpu.SemaphoreType.DMA((parts,)),
        ],
        compiler_params=params(),
        name="finish",
    )(q_pieces, gram, left, merged)
    return error_new, own_q.T


def solution(mesh, sizes=(8, 8, 4, 2)):
    finer = Mesh(mesh.devices.reshape(sizes), ("y", "z", "x", "c"))
    everyone = ("y", "z", "x", "c")
    in_specs = (P(DP, TENSOR), P(DP, TENSOR), P(everyone, None), P(), P())
    out_specs = (P(everyone, None), P(TENSOR, None))
    return jax.shard_map(
        body, mesh=finer, in_specs=in_specs, out_specs=out_specs, check_vma=False
    )
```

```python
import functools

import jax
import jax.numpy as jnp
from jax import lax
from jax.experimental import pallas as pl
from jax.experimental.pallas import tpu as pltpu
from jax.sharding import Mesh
from jax.sharding import PartitionSpec as P

DP = ("y", "z")
TENSOR = ("x", "c")
CHUNK = 256
LANES = 128
BLOCKS = 5
MIB = 1024 * 1024
F32 = jnp.float32
BF16 = jnp.bfloat16


def dot(a, b, contract, precision=None):
    return lax.dot_general(
        a, b, (contract, ((), ())), precision=precision, preferred_element_type=F32
    )


def params(limit=20 * MIB):
    return pltpu.CompilerParams(vmem_limit_bytes=limit)


def split(x):
    high = x.astype(BF16)
    return high, (x - high.astype(F32)).astype(BF16)


def kept_ranks(pauses, row_count):
    count = pauses.shape[0]
    row = lax.broadcasted_iota(jnp.int32, (count, count), 0)
    col = lax.broadcasted_iota(jnp.int32, (count, count), 1)
    wide = pauses.astype(F32).reshape(1, count)
    column = jnp.sum(jnp.where(row == col, wide, 0.0), axis=1, keepdims=True)
    spot = lax.broadcasted_iota(jnp.int32, (1, row_count), 1).astype(F32)
    before = jnp.sum(jnp.where(column < spot, 1.0, 0.0), axis=0, keepdims=True)
    struck = jnp.sum(jnp.where(column == spot, 1.0, 0.0), axis=0, keepdims=True)
    return jnp.where(struck > 0.0, -1.0, spot - before)


def kept_rows(pauses, values_ref, kept_count):
    row_count = values_ref.shape[0]
    ranks = kept_ranks(pauses, row_count)
    size = kept_count // BLOCKS
    window = size + row_count - kept_count
    blocks = []
    for block in range(BLOCKS):
        start = block * size
        here = ranks if start == 0 else pltpu.roll(ranks, row_count - start, 1)
        rank = lax.broadcasted_iota(jnp.int32, (size, window), 0) + start
        pick = jnp.where(rank.astype(F32) == here[:, :window], 1.0, 0.0).astype(BF16)
        blocks.append(dot(pick, values_ref[start : start + window], ((1,), (0,))))
    return jnp.concatenate(blocks, axis=0)


def compact_cotangents_kernel(pause_ref, cot_ref, out_ref):
    kept = kept_rows(pause_ref[...], cot_ref, out_ref.shape[1]).astype(BF16)
    for copy in range(out_ref.shape[0]):
        out_ref[copy] = kept


def compact_features_kernel(kept_count, pause_ref, act_ref, out_ref):
    kept = kept_rows(pause_ref[...], act_ref, kept_count)
    spare = jnp.zeros((out_ref.shape[1] - kept_count, kept.shape[1]), F32)
    out_ref[...] = jnp.concatenate([kept, spare], axis=0).T.astype(BF16)


def merge_kernel(feat_ref, own_ref, other_ref, err_ref, q_ref, merged_ref, left_ref):
    first = lax.axis_index("c") == 0
    pieces, kept_count, lanes = own_ref.shape
    rank = q_ref.shape[0]
    features, padded_count = feat_ref.shape
    q_high, q_low = split(q_ref[...])
    total = jnp.zeros((features, LANES), F32)
    for piece in range(pieces):
        own, other = own_ref[piece], other_ref[piece]
        cots = jnp.concatenate([jnp.where(first, own, other), jnp.where(first, other, own)], axis=1)
        cots = jnp.concatenate([cots, jnp.zeros((padded_count - kept_count, CHUNK), BF16)], axis=0)
        here = slice(piece * CHUNK, (piece + 1) * CHUNK)
        merged = dot(feat_ref[...], cots, ((1,), (0,))) + err_ref[:, here].astype(F32)
        merged_ref[:, here] = merged
        m_high, m_low = split(merged)
        high, low = q_high[:, here], q_low[:, here]
        upper = jnp.concatenate([high, high], axis=1)
        lower = jnp.concatenate([low, jnp.zeros_like(low)], axis=1)
        spare = jnp.zeros((LANES - 2 * rank, 2 * CHUNK), BF16)
        total += dot(
            jnp.concatenate([m_high, m_low], axis=1),
            jnp.concatenate([upper, lower, spare], axis=0),
            ((1,), (1,)),
        )
    turned = total.T
    left = (turned[:rank] + turned[rank : 2 * rank]).astype(BF16)
    for copy in range(left_ref.shape[0]):
        left_ref[copy] = left


def add_copies_kernel(in_ref, out_ref):
    total = in_ref[0].astype(F32)
    for copy in range(1, in_ref.shape[0]):
        total += in_ref[copy].astype(F32)
    total = total.astype(out_ref.dtype)
    for copy in range(out_ref.shape[0]):
        out_ref[copy] = total


def pack(gram, lines):
    rank = gram.shape[0]
    wide = jnp.concatenate([gram, jnp.zeros((rank, LANES - rank), F32)], axis=1)
    total = wide[:lines]
    for block in range(1, rank // lines):
        total += pltpu.roll(wide[block * lines : (block + 1) * lines], block * rank, 1)
    return total


def unpack(packed, rank):
    lines = packed.shape[0]
    blocks = [packed[:, :rank]]
    for block in range(1, rank // lines):
        blocks.append(pltpu.roll(packed, LANES - block * rank, 1)[:, :rank])
    return jnp.concatenate(blocks, axis=0)


def project_kernel(replicas, in_ref, merged_ref, left_ref, out_ref):
    rank = left_ref.shape[0]
    pieces, lines, lanes = out_ref.shape
    wide = CHUNK // lanes
    total = in_ref[0].astype(F32)
    for copy in range(1, in_ref.shape[0]):
        total += in_ref[copy].astype(F32)
    total = total / replicas
    left_ref[...] = total
    high, low = split(total)
    stack = jnp.concatenate([high, low], axis=0)
    gram = dot(total, total, ((1,), (1,)), lax.Precision.HIGHEST)
    packed = pack(gram, lines - rank)
    for chunk in range(pieces // wide):
        m_high, m_low = split(merged_ref[:, chunk * CHUNK : (chunk + 1) * CHUNK])
        both = dot(stack, m_high, ((1,), (0,)))
        part = both[:rank] + both[rank:] + dot(high, m_low, ((1,), (0,)))
        for piece in range(wide):
            here = chunk * wide + piece
            out_ref[here, :rank] = part[:, piece * lanes : (piece + 1) * lanes]
            out_ref[here, rank:] = packed


def add_blocks_kernel(rank, in_ref, out_ref, gram_ref):
    total = in_ref[0]
    for copy in range(1, in_ref.shape[0]):
        total += in_ref[copy]
    for copy in range(out_ref.shape[0]):
        out_ref[copy] = total[:rank].astype(out_ref.dtype)
    gram_ref[...] = total[rank:]


def inverse_factor(gram):
    rank = gram.shape[0]
    row = lax.broadcasted_iota(jnp.int32, (rank, rank), 0)
    col = lax.broadcasted_iota(jnp.int32, (rank, rank), 1)
    spare = jnp.zeros((rank, LANES - 2 * rank), F32)
    table = jnp.concatenate([jnp.where(row == col, 1.0, 0.0), gram, spare], axis=1)
    line = lax.broadcasted_iota(jnp.int32, (rank, LANES), 0)
    pivots = jnp.ones((rank, LANES), F32)
    for k in range(0, rank, 2):
        at = rank + k
        column = jnp.broadcast_to(table[:, at : at + 1], (rank, LANES))
        second = jnp.broadcast_to(table[:, at + 1 : at + 2], (rank, LANES))
        pivot = column[k : k + 1]
        inverse = 1.0 / pivot
        slope = column[k + 1 : k + 2] * inverse
        after = second[k + 1 : k + 2] - slope * second[k : k + 1]
        top = table[k : k + 1]
        bottom = table[k + 1 : k + 2] - slope * top
        below = line > k + 1
        upper = jnp.where(below, column * inverse, 0.0)
        lower = jnp.where(below, second - slope * column, 0.0) * (1.0 / after)
        table = jnp.where(line == k + 1, bottom, table - upper * top - lower * bottom)
        pivots = jnp.where(line == k, pivot, jnp.where(line == k + 1, after, pivots))
    return (table / jnp.sqrt(pivots))[:, :rank]


def finish_kernel(replicas, in_ref, gram_ref, left_ref, merged_ref, err_hbm, own_ref, q_ref, err_ref, sems):
    rank, width = q_ref.shape
    inverse = inverse_factor(unpack(gram_ref[...], rank))
    raw = jnp.concatenate([in_ref[piece] for piece in range(in_ref.shape[0])], axis=1)
    raw = raw / replicas
    q_ref[...] = raw
    lanes = own_ref.shape[1]
    place = lax.axis_index("x") * lax.axis_size("c") + lax.axis_index("c")
    own = q_ref[:, pl.ds(pl.multiple_of(place * lanes, lanes), lanes)]
    own_ref[...] = dot(inverse, own, ((1,), (0,)), lax.Precision.HIGHEST)
    square = dot(inverse.T, inverse, ((1,), (0,)), lax.Precision.HIGHEST)
    high, low = split(dot(square, raw, ((1,), (0,)), lax.Precision.HIGHEST))
    stack = jnp.concatenate([high, high, low, jnp.zeros_like(high)], axis=0)
    high, low = split(left_ref[...])
    high = high.astype(F32)
    low = low.astype(F32)
    turned = jnp.concatenate([high, low, high, jnp.zeros_like(high)], axis=0).T.astype(BF16)
    stores = []
    chunks, rows, _ = err_ref.shape
    for chunk in range(chunks):
        here = slice(chunk * rows, (chunk + 1) * rows)
        update = dot(turned[here], stack, ((1,), (0,)))
        err_ref[chunk] = (merged_ref[here] - update).astype(BF16)
        stores.append(
            pltpu.make_async_copy(
                err_ref.at[chunk], err_hbm.at[pl.ds(chunk * rows, rows)], sems.at[chunk]
            )
        )
        stores[-1].start()
    for store in stores:
        store.wait()


def in_hbm():
    return pl.BlockSpec(memory_space=pltpu.HBM)


def whole(shape):
    return pl.BlockSpec(shape, lambda *_: (0,) * len(shape))


def to_column(pieces, turn):
    axes = ("y", "z", "c")
    ny, nz, nc = (lax.axis_size(axis) for axis in axes)
    groups = []
    for core in range(nc):
        if (core + turn) % 2 == 0:
            groups += [[(y * nz + z) * nc + core for z in range(nz)] for y in range(ny)]
        else:
            groups += [[(y * nz + z) * nc + core for y in range(ny)] for z in range(nz)]
    return lax.all_to_all(
        pieces, axes, split_axis=0, concat_axis=0, tiled=True, axis_index_groups=groups
    )


def to_all(pieces, axes):
    return lax.all_to_all(pieces, axes, split_axis=0, concat_axis=0, tiled=True)


def add_copies(x, count, dtype):
    return pl.pallas_call(
        add_copies_kernel,
        out_shape=jax.ShapeDtypeStruct((count, *x.shape[1:]), dtype),
        compiler_params=params(),
        name="add_copies",
    )(x)


def body(activations, cotangents, error_old, pause_positions, initial_q):
    row_count, features = activations.shape
    lanes = cotangents.shape[1]
    width, rank = initial_q.shape
    kept_count = row_count - pause_positions.shape[0]
    padded_count = -(-kept_count // CHUNK) * CHUNK
    replicas = lax.axis_size(DP)
    line_x, across = lax.axis_size("x"), lax.axis_size("z")
    crowd = lax.axis_size(TENSOR)
    chunks = width // CHUNK
    lines = rank * rank // LANES
    pauses = pause_positions

    cot_copies = pl.pallas_call(
        compact_cotangents_kernel,
        out_shape=jax.ShapeDtypeStruct((line_x, kept_count, lanes), BF16),
        compiler_params=params(),
        name="compact_cotangents",
    )(pauses, cotangents)
    own = to_all(cot_copies, "x")
    kept_features = pl.pallas_call(
        functools.partial(compact_features_kernel, kept_count),
        out_shape=jax.ShapeDtypeStruct((features, padded_count), BF16),
        compiler_params=params(),
        cost_estimate=pl.CostEstimate(
            flops=2 * kept_count * row_count * features,
            bytes_accessed=4 * row_count * features,
            transcendentals=0,
        ),
        name="compact_features",
    )(pauses, activations)
    cores = lax.axis_size("c")
    other = lax.ppermute(own, "c", [(i, cores - 1 - i) for i in range(cores)])

    merged, left_copies = pl.pallas_call(
        merge_kernel,
        out_shape=[
            jax.ShapeDtypeStruct((features, width), F32),
            jax.ShapeDtypeStruct((across, rank, features), BF16),
        ],
        compiler_params=params(),
        name="merge",
    )(kept_features, own, other, error_old, initial_q.T)

    left_copies = add_copies(to_column(left_copies, 0), lax.axis_size("y"), BF16)
    left_copies = to_column(left_copies, 1)

    left, q_pieces = pl.pallas_call(
        functools.partial(project_kernel, replicas),
        out_shape=[
            jax.ShapeDtypeStruct((rank, features), F32),
            jax.ShapeDtypeStruct((crowd, rank + lines, lanes), F32),
        ],
        compiler_params=params(),
        name="project",
    )(left_copies, merged)

    q_copies, gram = pl.pallas_call(
        functools.partial(add_blocks_kernel, rank),
        out_shape=[
            jax.ShapeDtypeStruct((across, rank, lanes), BF16),
            jax.ShapeDtypeStruct((lines, lanes), F32),
        ],
        compiler_params=params(),
        name="add_blocks",
    )(to_all(q_pieces, TENSOR))
    q_copies = add_copies(to_column(q_copies, 0), lax.axis_size("y"), F32)
    q_copies = add_copies(to_column(q_copies, 1), crowd, F32)
    q_pieces = to_all(q_copies, TENSOR)

    parts = features // LANES
    error_new, own_q = pl.pallas_call(
        functools.partial(finish_kernel, replicas),
        out_specs=[in_hbm(), whole((rank, lanes))],
        out_shape=[
            jax.ShapeDtypeStruct((features, width), BF16),
            jax.ShapeDtypeStruct((rank, lanes), F32),
        ],
        scratch_shapes=[
            pltpu.VMEM((rank, width), F32),
            pltpu.VMEM((parts, LANES, width), BF16),
            pltpu.SemaphoreType.DMA((parts,)),
        ],
        compiler_params=params(),
        name="finish",
    )(q_pieces, gram, left, merged)
    return error_new, own_q.T


def solution(mesh, sizes=(8, 8, 4, 2)):
    finer = Mesh(mesh.devices.reshape(sizes), ("y", "z", "x", "c"))
    everyone = ("y", "z", "x", "c")
    in_specs = (P(DP, TENSOR), P(DP, TENSOR), P(everyone, None), P(), P())
    out_specs = (P(everyone, None), P(TENSOR, None))
    return jax.shard_map(
        body, mesh=finer, in_specs=in_specs, out_specs=out_specs, check_vma=False
    )
```

```python
import functools

import jax
import jax.numpy as jnp
from jax import lax
from jax.experimental import pallas as pl
from jax.experimental.pallas import tpu as pltpu
from jax.sharding import Mesh
from jax.sharding import PartitionSpec as P

DP = ("y", "z")
TENSOR = ("x", "c")
CHUNK = 256
LANES = 128
BLOCKS = 5
MIB = 1024 * 1024
F32 = jnp.float32
BF16 = jnp.bfloat16


def dot(a, b, contract, precision=None):
    return lax.dot_general(
        a, b, (contract, ((), ())), precision=precision, preferred_element_type=F32
    )


def params(limit=20 * MIB):
    return pltpu.CompilerParams(vmem_limit_bytes=limit)


def split(x):
    high = x.astype(BF16)
    return high, (x - high.astype(F32)).astype(BF16)


def kept_ranks(pauses, row_count):
    count = pauses.shape[0]
    row = lax.broadcasted_iota(jnp.int32, (count, count), 0)
    col = lax.broadcasted_iota(jnp.int32, (count, count), 1)
    wide = pauses.astype(F32).reshape(1, count)
    column = jnp.sum(jnp.where(row == col, wide, 0.0), axis=1, keepdims=True)
    spot = lax.broadcasted_iota(jnp.int32, (1, row_count), 1).astype(F32)
    before = jnp.sum(jnp.where(column < spot, 1.0, 0.0), axis=0, keepdims=True)
    struck = jnp.sum(jnp.where(column == spot, 1.0, 0.0), axis=0, keepdims=True)
    return jnp.where(struck > 0.0, -1.0, spot - before)


def kept_rows(pauses, values_ref, kept_count):
    row_count = values_ref.shape[0]
    ranks = kept_ranks(pauses, row_count)
    size = kept_count // BLOCKS
    window = size + row_count - kept_count
    blocks = []
    for block in range(BLOCKS):
        start = block * size
        here = ranks if start == 0 else pltpu.roll(ranks, row_count - start, 1)
        rank = lax.broadcasted_iota(jnp.int32, (size, window), 0) + start
        pick = jnp.where(rank.astype(F32) == here[:, :window], 1.0, 0.0).astype(BF16)
        blocks.append(dot(pick, values_ref[start : start + window], ((1,), (0,))))
    return jnp.concatenate(blocks, axis=0)


def compact_cotangents_kernel(pause_ref, cot_ref, out_ref):
    kept = kept_rows(pause_ref[...], cot_ref, out_ref.shape[1]).astype(BF16)
    for copy in range(out_ref.shape[0]):
        out_ref[copy] = kept


def compact_features_kernel(kept_count, pause_ref, act_ref, out_ref):
    kept = kept_rows(pause_ref[...], act_ref, kept_count)
    spare = jnp.zeros((out_ref.shape[1] - kept_count, kept.shape[1]), F32)
    out_ref[...] = jnp.concatenate([kept, spare], axis=0).T.astype(BF16)


def places(side, pieces, lanes):
    core = lax.axis_index("c")
    core = core if side == 0 else 1 - core
    return [pl.multiple_of((2 * piece + core) * lanes, lanes) for piece in range(pieces)]


def at_places(ref, starts, lanes):
    return jnp.concatenate([ref[:, pl.ds(start, lanes)] for start in starts], axis=1)


def merge_part(side, feat_ref, cot_ref, err_ref, q_ref, merged_ref):
    pieces, kept_count, lanes = cot_ref.shape
    rank = q_ref.shape[0]
    features, padded_count = feat_ref.shape
    wide = CHUNK // lanes
    starts = places(side, pieces, lanes)
    total = jnp.zeros((features, LANES), F32)
    for chunk in range(pieces // wide):
        group = range(chunk * wide, (chunk + 1) * wide)
        spots = [starts[piece] for piece in group]
        cots = jnp.concatenate([cot_ref[piece] for piece in group], axis=1)
        cots = jnp.concatenate([cots, jnp.zeros((padded_count - kept_count, CHUNK), BF16)], axis=0)
        old = at_places(err_ref, spots, lanes).astype(F32)
        merged = dot(feat_ref[...], cots, ((1,), (0,))) + old
        merged_ref[:, chunk * CHUNK : (chunk + 1) * CHUNK] = merged
        m_high, m_low = split(merged)
        high, low = split(at_places(q_ref, spots, lanes))
        upper = jnp.concatenate([high, high], axis=1)
        lower = jnp.concatenate([low, jnp.zeros_like(low)], axis=1)
        spare = jnp.zeros((LANES - 2 * rank, 2 * CHUNK), BF16)
        total += dot(
            jnp.concatenate([m_high, m_low], axis=1),
            jnp.concatenate([upper, lower, spare], axis=0),
            ((1,), (1,)),
        )
    return total


def merge_own_kernel(feat_ref, own_ref, err_ref, q_ref, merged_ref, total_ref):
    total_ref[...] = merge_part(0, feat_ref, own_ref, err_ref, q_ref, merged_ref)


def merge_other_kernel(feat_ref, other_ref, err_ref, q_ref, total_ref, merged_ref, left_ref):
    rank = q_ref.shape[0]
    total = total_ref[...] + merge_part(1, feat_ref, other_ref, err_ref, q_ref, merged_ref)
    turned = total.T
    left = (turned[:rank] + turned[rank : 2 * rank]).astype(BF16)
    for copy in range(left_ref.shape[0]):
        left_ref[copy] = left


def add_copies_kernel(in_ref, out_ref):
    total = in_ref[0].astype(F32)
    for copy in range(1, in_ref.shape[0]):
        total += in_ref[copy].astype(F32)
    total = total.astype(out_ref.dtype)
    for copy in range(out_ref.shape[0]):
        out_ref[copy] = total


def pack(gram, lines):
    rank = gram.shape[0]
    wide = jnp.concatenate([gram, jnp.zeros((rank, LANES - rank), F32)], axis=1)
    total = wide[:lines]
    for block in range(1, rank // lines):
        total += pltpu.roll(wide[block * lines : (block + 1) * lines], block * rank, 1)
    return total


def unpack(packed, rank):
    lines = packed.shape[0]
    blocks = [packed[:, :rank]]
    for block in range(1, rank // lines):
        blocks.append(pltpu.roll(packed, LANES - block * rank, 1)[:, :rank])
    return jnp.concatenate(blocks, axis=0)


def project_kernel(replicas, in_ref, own_ref, other_ref, left_ref, out_ref):
    rank = left_ref.shape[0]
    pieces, lines, lanes = out_ref.shape
    wide = CHUNK // lanes
    total = in_ref[0].astype(F32)
    for copy in range(1, in_ref.shape[0]):
        total += in_ref[copy].astype(F32)
    total = total / replicas
    left_ref[...] = total
    high, low = split(total)
    stack = jnp.concatenate([high, low], axis=0)
    gram = dot(total, total, ((1,), (1,)), lax.Precision.HIGHEST)
    packed = pack(gram, lines - rank)
    for side, merged_ref in enumerate((own_ref, other_ref)):
        core = lax.axis_index("c")
        core = core if side == 0 else 1 - core
        for chunk in range(merged_ref.shape[1] // CHUNK):
            m_high, m_low = split(merged_ref[:, chunk * CHUNK : (chunk + 1) * CHUNK])
            both = dot(stack, m_high, ((1,), (0,)))
            part = both[:rank] + both[rank:] + dot(high, m_low, ((1,), (0,)))
            for piece in range(wide):
                here = 2 * (chunk * wide + piece) + core
                out_ref[here, :rank] = part[:, piece * lanes : (piece + 1) * lanes]
                out_ref[here, rank:] = packed


def add_blocks_kernel(rank, in_ref, out_ref, gram_ref):
    total = in_ref[0]
    for copy in range(1, in_ref.shape[0]):
        total += in_ref[copy]
    for copy in range(out_ref.shape[0]):
        out_ref[copy] = total[:rank].astype(out_ref.dtype)
    gram_ref[...] = total[rank:]


def inverse_factor(gram):
    rank = gram.shape[0]
    row = lax.broadcasted_iota(jnp.int32, (rank, rank), 0)
    col = lax.broadcasted_iota(jnp.int32, (rank, rank), 1)
    spare = jnp.zeros((rank, LANES - 2 * rank), F32)
    table = jnp.concatenate([jnp.where(row == col, 1.0, 0.0), gram, spare], axis=1)
    line = lax.broadcasted_iota(jnp.int32, (rank, LANES), 0)
    pivots = jnp.ones((rank, LANES), F32)
    for k in range(0, rank, 2):
        at = rank + k
        column = jnp.broadcast_to(table[:, at : at + 1], (rank, LANES))
        second = jnp.broadcast_to(table[:, at + 1 : at + 2], (rank, LANES))
        pivot = column[k : k + 1]
        inverse = 1.0 / pivot
        slope = column[k + 1 : k + 2] * inverse
        after = second[k + 1 : k + 2] - slope * second[k : k + 1]
        top = table[k : k + 1]
        bottom = table[k + 1 : k + 2] - slope * top
        below = line > k + 1
        upper = jnp.where(below, column * inverse, 0.0)
        lower = jnp.where(below, second - slope * column, 0.0) * (1.0 / after)
        table = jnp.where(line == k + 1, bottom, table - upper * top - lower * bottom)
        pivots = jnp.where(line == k, pivot, jnp.where(line == k + 1, after, pivots))
    return (table / jnp.sqrt(pivots))[:, :rank]


def finish_kernel(
    replicas,
    in_ref,
    gram_ref,
    left_ref,
    own_merged_ref,
    other_merged_ref,
    err_hbm,
    own_ref,
    q_ref,
    stack_ref,
    err_ref,
    sems,
):
    rank, width = q_ref.shape
    inverse = inverse_factor(unpack(gram_ref[...], rank))
    raw = jnp.concatenate([in_ref[piece] for piece in range(in_ref.shape[0])], axis=1)
    raw = raw / replicas
    q_ref[...] = raw
    lanes = own_ref.shape[1]
    place = lax.axis_index("x") * lax.axis_size("c") + lax.axis_index("c")
    own = q_ref[:, pl.ds(pl.multiple_of(place * lanes, lanes), lanes)]
    own_ref[...] = dot(inverse, own, ((1,), (0,)), lax.Precision.HIGHEST)
    square = dot(inverse.T, inverse, ((1,), (0,)), lax.Precision.HIGHEST)
    high, low = split(dot(square, raw, ((1,), (0,)), lax.Precision.HIGHEST))
    stack_ref[...] = jnp.concatenate([high, high, low, jnp.zeros_like(high)], axis=0)
    high, low = split(left_ref[...])
    high = high.astype(F32)
    low = low.astype(F32)
    turned = jnp.concatenate([high, low, high, jnp.zeros_like(high)], axis=0).T.astype(BF16)
    sides = []
    for side, merged_ref in enumerate((own_merged_ref, other_merged_ref)):
        starts = places(side, merged_ref.shape[1] // lanes, lanes)
        sides.append((merged_ref, starts, at_places(stack_ref, starts, lanes)))
    stores = []
    chunks, rows, _ = err_ref.shape
    for chunk in range(chunks):
        here = slice(chunk * rows, (chunk + 1) * rows)
        for merged_ref, starts, stack in sides:
            fresh = merged_ref[here] - dot(turned[here], stack, ((1,), (0,)))
            for piece, start in enumerate(starts):
                block = fresh[:, piece * lanes : (piece + 1) * lanes].astype(BF16)
                err_ref[chunk, :, pl.ds(start, lanes)] = block
        stores.append(
            pltpu.make_async_copy(
                err_ref.at[chunk], err_hbm.at[pl.ds(chunk * rows, rows)], sems.at[chunk]
            )
        )
        stores[-1].start()
    for store in stores:
        store.wait()


def in_hbm():
    return pl.BlockSpec(memory_space=pltpu.HBM)


def whole(shape):
    return pl.BlockSpec(shape, lambda *_: (0,) * len(shape))


def to_column(pieces, turn):
    axes = ("y", "z", "c")
    ny, nz, nc = (lax.axis_size(axis) for axis in axes)
    groups = []
    for core in range(nc):
        if (core + turn) % 2 == 0:
            groups += [[(y * nz + z) * nc + core for z in range(nz)] for y in range(ny)]
        else:
            groups += [[(y * nz + z) * nc + core for y in range(ny)] for z in range(nz)]
    return lax.all_to_all(
        pieces, axes, split_axis=0, concat_axis=0, tiled=True, axis_index_groups=groups
    )


def to_all(pieces, axes):
    return lax.all_to_all(pieces, axes, split_axis=0, concat_axis=0, tiled=True)


def add_copies(x, count, dtype):
    return pl.pallas_call(
        add_copies_kernel,
        out_shape=jax.ShapeDtypeStruct((count, *x.shape[1:]), dtype),
        compiler_params=params(),
        name="add_copies",
    )(x)


def body(activations, cotangents, error_old, pause_positions, initial_q):
    row_count, features = activations.shape
    lanes = cotangents.shape[1]
    width, rank = initial_q.shape
    kept_count = row_count - pause_positions.shape[0]
    padded_count = -(-kept_count // CHUNK) * CHUNK
    replicas = lax.axis_size(DP)
    line_x, across = lax.axis_size("x"), lax.axis_size("z")
    crowd = lax.axis_size(TENSOR)
    lines = rank * rank // LANES
    pauses = pause_positions

    cot_copies = pl.pallas_call(
        compact_cotangents_kernel,
        out_shape=jax.ShapeDtypeStruct((line_x, kept_count, lanes), BF16),
        compiler_params=params(),
        name="compact_cotangents",
    )(pauses, cotangents)
    own = to_all(cot_copies, "x")
    kept_features = pl.pallas_call(
        functools.partial(compact_features_kernel, kept_count),
        out_shape=jax.ShapeDtypeStruct((features, padded_count), BF16),
        compiler_params=params(),
        cost_estimate=pl.CostEstimate(
            flops=2 * kept_count * row_count * features,
            bytes_accessed=4 * row_count * features,
            transcendentals=0,
        ),
        name="compact_features",
    )(pauses, activations)
    cores = lax.axis_size("c")
    other = lax.ppermute(own, "c", [(i, cores - 1 - i) for i in range(cores)])

    turned_q = initial_q.T
    merged_own, total = pl.pallas_call(
        merge_own_kernel,
        out_shape=[
            jax.ShapeDtypeStruct((features, width // cores), F32),
            jax.ShapeDtypeStruct((features, LANES), F32),
        ],
        compiler_params=params(),
        cost_estimate=pl.CostEstimate(
            flops=2 * features * padded_count * width // cores,
            bytes_accessed=6 * features * width // cores,
            transcendentals=0,
        ),
        name="merge_own",
    )(kept_features, own, error_old, turned_q)
    merged_other, left_copies = pl.pallas_call(
        merge_other_kernel,
        out_shape=[
            jax.ShapeDtypeStruct((features, width // cores), F32),
            jax.ShapeDtypeStruct((across, rank, features), BF16),
        ],
        compiler_params=params(),
        name="merge_other",
    )(kept_features, other, error_old, turned_q, total)

    left_copies = add_copies(to_column(left_copies, 0), lax.axis_size("y"), BF16)
    left_copies = to_column(left_copies, 1)

    left, q_pieces = pl.pallas_call(
        functools.partial(project_kernel, replicas),
        out_shape=[
            jax.ShapeDtypeStruct((rank, features), F32),
            jax.ShapeDtypeStruct((crowd, rank + lines, lanes), F32),
        ],
        compiler_params=params(),
        name="project",
    )(left_copies, merged_own, merged_other)

    q_copies, gram = pl.pallas_call(
        functools.partial(add_blocks_kernel, rank),
        out_shape=[
            jax.ShapeDtypeStruct((across, rank, lanes), BF16),
            jax.ShapeDtypeStruct((lines, lanes), F32),
        ],
        compiler_params=params(),
        name="add_blocks",
    )(to_all(q_pieces, TENSOR))
    q_copies = add_copies(to_column(q_copies, 0), lax.axis_size("y"), F32)
    q_copies = add_copies(to_column(q_copies, 1), crowd, F32)
    q_pieces = to_all(q_copies, TENSOR)

    parts = features // LANES
    error_new, own_q = pl.pallas_call(
        functools.partial(finish_kernel, replicas),
        out_specs=[in_hbm(), whole((rank, lanes))],
        out_shape=[
            jax.ShapeDtypeStruct((features, width), BF16),
            jax.ShapeDtypeStruct((rank, lanes), F32),
        ],
        scratch_shapes=[
            pltpu.VMEM((rank, width), F32),
            pltpu.VMEM((4 * rank, width), BF16),
            pltpu.VMEM((parts, LANES, width), BF16),
            pltpu.SemaphoreType.DMA((parts,)),
        ],
        compiler_params=params(),
        name="finish",
    )(q_pieces, gram, left, merged_own, merged_other)
    return error_new, own_q.T


def solution(mesh, sizes=(8, 8, 4, 2)):
    finer = Mesh(mesh.devices.reshape(sizes), ("y", "z", "x", "c"))
    everyone = ("y", "z", "x", "c")
    in_specs = (P(DP, TENSOR), P(DP, TENSOR), P(everyone, None), P(), P())
    out_specs = (P(everyone, None), P(TENSOR, None))
    return jax.shard_map(
        body, mesh=finer, in_specs=in_specs, out_specs=out_specs, check_vma=False
    )
```

```python
import functools

import jax
import jax.numpy as jnp
from jax import lax
from jax.experimental import pallas as pl
from jax.experimental.pallas import tpu as pltpu
from jax.sharding import Mesh
from jax.sharding import PartitionSpec as P

DP = ("y", "z")
TENSOR = ("x", "c")
CHUNK = 256
LANES = 128
BLOCKS = 5
MIB = 1024 * 1024
F32 = jnp.float32
BF16 = jnp.bfloat16


def dot(a, b, contract, precision=None):
    return lax.dot_general(
        a, b, (contract, ((), ())), precision=precision, preferred_element_type=F32
    )


def params(limit=20 * MIB):
    return pltpu.CompilerParams(vmem_limit_bytes=limit)


def split(x):
    high = x.astype(BF16)
    return high, (x - high.astype(F32)).astype(BF16)


def kept_ranks(pauses, row_count):
    count = pauses.shape[0]
    row = lax.broadcasted_iota(jnp.int32, (count, count), 0)
    col = lax.broadcasted_iota(jnp.int32, (count, count), 1)
    wide = pauses.astype(F32).reshape(1, count)
    column = jnp.sum(jnp.where(row == col, wide, 0.0), axis=1, keepdims=True)
    spot = lax.broadcasted_iota(jnp.int32, (1, row_count), 1).astype(F32)
    before = jnp.sum(jnp.where(column < spot, 1.0, 0.0), axis=0, keepdims=True)
    struck = jnp.sum(jnp.where(column == spot, 1.0, 0.0), axis=0, keepdims=True)
    return jnp.where(struck > 0.0, -1.0, spot - before)


def kept_rows(ranks, values_ref, kept_count):
    row_count = values_ref.shape[0]
    size = kept_count // BLOCKS
    window = size + row_count - kept_count
    blocks = []
    for block in range(BLOCKS):
        start = block * size
        here = ranks if start == 0 else pltpu.roll(ranks, row_count - start, 1)
        rank = lax.broadcasted_iota(jnp.int32, (size, window), 0) + start
        pick = jnp.where(rank.astype(F32) == here[:, :window], 1.0, 0.0).astype(BF16)
        blocks.append(dot(pick, values_ref[start : start + window], ((1,), (0,))))
    return jnp.concatenate(blocks, axis=0)


def compact_cotangents_kernel(pause_hbm, cot_hbm, out_ref, pause_ref, cot_ref, sems):
    pauses = pltpu.make_async_copy(pause_hbm, pause_ref, sems.at[0])
    cots = pltpu.make_async_copy(cot_hbm, cot_ref, sems.at[1])
    pauses.start()
    cots.start()
    pauses.wait()
    ranks = kept_ranks(pause_ref[...], cot_ref.shape[0])
    cots.wait()
    kept = kept_rows(ranks, cot_ref, out_ref.shape[1]).astype(BF16)
    for copy in range(out_ref.shape[0]):
        out_ref[copy] = kept


def compact_features_kernel(kept_count, pause_ref, act_ref, out_ref):
    ranks = kept_ranks(pause_ref[...], act_ref.shape[0])
    kept = kept_rows(ranks, act_ref, kept_count)
    spare = jnp.zeros((out_ref.shape[1] - kept_count, kept.shape[1]), F32)
    out_ref[...] = jnp.concatenate([kept, spare], axis=0).T.astype(BF16)


def places(side, pieces, lanes):
    core = lax.axis_index("c")
    core = core if side == 0 else 1 - core
    return [pl.multiple_of((2 * piece + core) * lanes, lanes) for piece in range(pieces)]


def at_places(ref, starts, lanes):
    return jnp.concatenate([ref[:, pl.ds(start, lanes)] for start in starts], axis=1)


def merge_part(side, feat_ref, cot_ref, err_ref, q_ref, merged_ref):
    pieces, kept_count, lanes = cot_ref.shape
    rank = q_ref.shape[0]
    features, padded_count = feat_ref.shape
    wide = CHUNK // lanes
    starts = places(side, pieces, lanes)
    total = jnp.zeros((features, LANES), F32)
    for chunk in range(pieces // wide):
        group = range(chunk * wide, (chunk + 1) * wide)
        spots = [starts[piece] for piece in group]
        cots = jnp.concatenate([cot_ref[piece] for piece in group], axis=1)
        cots = jnp.concatenate([cots, jnp.zeros((padded_count - kept_count, CHUNK), BF16)], axis=0)
        old = at_places(err_ref, spots, lanes).astype(F32)
        merged = dot(feat_ref[...], cots, ((1,), (0,))) + old
        merged_ref[:, chunk * CHUNK : (chunk + 1) * CHUNK] = merged
        m_high, m_low = split(merged)
        high, low = split(at_places(q_ref, spots, lanes))
        upper = jnp.concatenate([high, high], axis=1)
        lower = jnp.concatenate([low, jnp.zeros_like(low)], axis=1)
        spare = jnp.zeros((LANES - 2 * rank, 2 * CHUNK), BF16)
        total += dot(
            jnp.concatenate([m_high, m_low], axis=1),
            jnp.concatenate([upper, lower, spare], axis=0),
            ((1,), (1,)),
        )
    return total


def merge_own_kernel(feat_ref, own_ref, err_ref, q_ref, merged_ref, total_ref):
    total_ref[...] = merge_part(0, feat_ref, own_ref, err_ref, q_ref, merged_ref)


def merge_other_kernel(feat_ref, other_ref, err_ref, q_ref, total_ref, merged_ref, left_ref):
    rank = q_ref.shape[0]
    total = total_ref[...] + merge_part(1, feat_ref, other_ref, err_ref, q_ref, merged_ref)
    turned = total.T
    left = (turned[:rank] + turned[rank : 2 * rank]).astype(BF16)
    for copy in range(left_ref.shape[0]):
        left_ref[copy] = left


def add_copies_kernel(in_ref, out_ref):
    total = in_ref[0].astype(F32)
    for copy in range(1, in_ref.shape[0]):
        total += in_ref[copy].astype(F32)
    total = total.astype(out_ref.dtype)
    for copy in range(out_ref.shape[0]):
        out_ref[copy] = total


def pack(gram, lines):
    rank = gram.shape[0]
    wide = jnp.concatenate([gram, jnp.zeros((rank, LANES - rank), F32)], axis=1)
    total = wide[:lines]
    for block in range(1, rank // lines):
        total += pltpu.roll(wide[block * lines : (block + 1) * lines], block * rank, 1)
    return total


def unpack(packed, rank):
    lines = packed.shape[0]
    blocks = [packed[:, :rank]]
    for block in range(1, rank // lines):
        blocks.append(pltpu.roll(packed, LANES - block * rank, 1)[:, :rank])
    return jnp.concatenate(blocks, axis=0)


def project_kernel(replicas, in_ref, own_ref, other_ref, left_ref, out_ref):
    rank = left_ref.shape[0]
    pieces, lines, lanes = out_ref.shape
    wide = CHUNK // lanes
    total = in_ref[0].astype(F32)
    for copy in range(1, in_ref.shape[0]):
        total += in_ref[copy].astype(F32)
    total = total / replicas
    left_ref[...] = total
    high, low = split(total)
    stack = jnp.concatenate([high, low], axis=0)
    gram = dot(total, total, ((1,), (1,)), lax.Precision.HIGHEST)
    packed = pack(gram, lines - rank)
    for side, merged_ref in enumerate((own_ref, other_ref)):
        core = lax.axis_index("c")
        core = core if side == 0 else 1 - core
        for chunk in range(merged_ref.shape[1] // CHUNK):
            m_high, m_low = split(merged_ref[:, chunk * CHUNK : (chunk + 1) * CHUNK])
            both = dot(stack, m_high, ((1,), (0,)))
            part = both[:rank] + both[rank:] + dot(high, m_low, ((1,), (0,)))
            for piece in range(wide):
                here = 2 * (chunk * wide + piece) + core
                out_ref[here, :rank] = part[:, piece * lanes : (piece + 1) * lanes]
                out_ref[here, rank:] = packed


def add_blocks_kernel(rank, in_ref, out_ref, gram_ref):
    total = in_ref[0]
    for copy in range(1, in_ref.shape[0]):
        total += in_ref[copy]
    for copy in range(out_ref.shape[0]):
        out_ref[copy] = total[:rank].astype(out_ref.dtype)
    gram_ref[...] = total[rank:]


def inverse_factor(gram):
    rank = gram.shape[0]
    row = lax.broadcasted_iota(jnp.int32, (rank, rank), 0)
    col = lax.broadcasted_iota(jnp.int32, (rank, rank), 1)
    diagonal = jnp.where(row == col, gram, 0.0)
    scale_row = 1.0 / jnp.sqrt(jnp.sum(diagonal, axis=0, keepdims=True))
    scale_column = 1.0 / jnp.sqrt(jnp.sum(diagonal, axis=1, keepdims=True))
    gram = gram * scale_row * scale_column
    spare = jnp.zeros((rank, LANES - 2 * rank), F32)
    table = jnp.concatenate([jnp.where(row == col, 1.0, 0.0), gram, spare], axis=1)
    line = lax.broadcasted_iota(jnp.int32, (rank, LANES), 0)
    pivots = jnp.ones((rank, LANES), F32)
    for k in range(0, rank, 2):
        at = rank + k
        column = jnp.broadcast_to(table[:, at : at + 1], (rank, LANES))
        second = jnp.broadcast_to(table[:, at + 1 : at + 2], (rank, LANES))
        pivot, cross = column[k : k + 1], second[k : k + 1]
        both = pivot * second[k + 1 : k + 2] - cross * cross
        inverse, inverse_both = 1.0 / pivot, 1.0 / both
        top = table[k : k + 1]
        bottom = table[k + 1 : k + 2] - cross * inverse * top
        below = line > k + 1
        upper = jnp.where(below, column * inverse, 0.0)
        lower = jnp.where(below, pivot * second - cross * column, 0.0) * inverse_both
        after = both * inverse
        table = jnp.where(line == k + 1, bottom, table - upper * top - lower * bottom)
        pivots = jnp.where(line == k, pivot, jnp.where(line == k + 1, after, pivots))
    return (table / jnp.sqrt(pivots))[:, :rank] * scale_row


def finish_kernel(
    replicas,
    in_ref,
    gram_ref,
    left_ref,
    own_merged_ref,
    other_merged_ref,
    err_hbm,
    own_ref,
    q_ref,
    stack_ref,
    err_ref,
    sems,
):
    rank, width = q_ref.shape
    inverse = inverse_factor(unpack(gram_ref[...], rank))
    raw = jnp.concatenate([in_ref[piece] for piece in range(in_ref.shape[0])], axis=1)
    raw = raw / replicas
    q_ref[...] = raw
    lanes = own_ref.shape[1]
    place = lax.axis_index("x") * lax.axis_size("c") + lax.axis_index("c")
    own = q_ref[:, pl.ds(pl.multiple_of(place * lanes, lanes), lanes)]
    own_ref[...] = dot(inverse, own, ((1,), (0,)), lax.Precision.HIGHEST)
    square = dot(inverse.T, inverse, ((1,), (0,)), lax.Precision.HIGHEST)
    high, low = split(dot(square, raw, ((1,), (0,)), lax.Precision.HIGHEST))
    stack_ref[...] = jnp.concatenate([high, high, low, jnp.zeros_like(high)], axis=0)
    high, low = split(left_ref[...])
    high = high.astype(F32)
    low = low.astype(F32)
    turned = jnp.concatenate([high, low, high, jnp.zeros_like(high)], axis=0).T.astype(BF16)
    sides = []
    for side, merged_ref in enumerate((own_merged_ref, other_merged_ref)):
        starts = places(side, merged_ref.shape[1] // lanes, lanes)
        sides.append((merged_ref, starts, at_places(stack_ref, starts, lanes)))
    stores = []
    chunks, rows, _ = err_ref.shape
    for chunk in range(chunks):
        here = slice(chunk * rows, (chunk + 1) * rows)
        for merged_ref, starts, stack in sides:
            fresh = merged_ref[here] - dot(turned[here], stack, ((1,), (0,)))
            for piece, start in enumerate(starts):
                block = fresh[:, piece * lanes : (piece + 1) * lanes].astype(BF16)
                err_ref[chunk, :, pl.ds(start, lanes)] = block
        stores.append(
            pltpu.make_async_copy(
                err_ref.at[chunk], err_hbm.at[pl.ds(chunk * rows, rows)], sems.at[chunk]
            )
        )
        stores[-1].start()
    for store in stores:
        store.wait()


def in_hbm():
    return pl.BlockSpec(memory_space=pltpu.HBM)


def kept_in_hbm(x):
    return pltpu.with_memory_space_constraint(x, pltpu.HBM)


def whole(shape):
    return pl.BlockSpec(shape, lambda *_: (0,) * len(shape))


def to_column(pieces, turn):
    axes = ("y", "z", "c")
    ny, nz, nc = (lax.axis_size(axis) for axis in axes)
    groups = []
    for core in range(nc):
        if (core + turn) % 2 == 0:
            groups += [[(y * nz + z) * nc + core for z in range(nz)] for y in range(ny)]
        else:
            groups += [[(y * nz + z) * nc + core for y in range(ny)] for z in range(nz)]
    return lax.all_to_all(
        pieces, axes, split_axis=0, concat_axis=0, tiled=True, axis_index_groups=groups
    )


def to_all(pieces, axes):
    return lax.all_to_all(pieces, axes, split_axis=0, concat_axis=0, tiled=True)


def add_copies(x, count, dtype):
    return pl.pallas_call(
        add_copies_kernel,
        out_shape=jax.ShapeDtypeStruct((count, *x.shape[1:]), dtype),
        compiler_params=params(),
        name="add_copies",
    )(x)


def body(activations, cotangents, error_old, pause_positions, initial_q):
    row_count, features = activations.shape
    lanes = cotangents.shape[1]
    width, rank = initial_q.shape
    kept_count = row_count - pause_positions.shape[0]
    padded_count = -(-kept_count // CHUNK) * CHUNK
    replicas = lax.axis_size(DP)
    line_x, across = lax.axis_size("x"), lax.axis_size("z")
    crowd = lax.axis_size(TENSOR)
    lines = rank * rank // LANES
    pauses = pause_positions

    cot_copies = pl.pallas_call(
        compact_cotangents_kernel,
        in_specs=[in_hbm(), in_hbm()],
        scratch_shapes=[
            pltpu.VMEM(pauses.shape, jnp.int32),
            pltpu.VMEM(cotangents.shape, BF16),
            pltpu.SemaphoreType.DMA((2,)),
        ],
        out_shape=jax.ShapeDtypeStruct((line_x, kept_count, lanes), BF16),
        compiler_params=params(),
        name="compact_cotangents",
    )(kept_in_hbm(pauses), kept_in_hbm(cotangents))
    own = to_all(cot_copies, "x")
    kept_features = pl.pallas_call(
        functools.partial(compact_features_kernel, kept_count),
        out_shape=jax.ShapeDtypeStruct((features, padded_count), BF16),
        compiler_params=params(),
        cost_estimate=pl.CostEstimate(
            flops=2 * kept_count * row_count * features,
            bytes_accessed=4 * row_count * features,
            transcendentals=0,
        ),
        name="compact_features",
    )(pauses, activations)
    cores = lax.axis_size("c")
    other = lax.ppermute(own, "c", [(i, cores - 1 - i) for i in range(cores)])

    turned_q = initial_q.T
    merged_own, total = pl.pallas_call(
        merge_own_kernel,
        out_shape=[
            jax.ShapeDtypeStruct((features, width // cores), F32),
            jax.ShapeDtypeStruct((features, LANES), F32),
        ],
        compiler_params=params(),
        cost_estimate=pl.CostEstimate(
            flops=2 * features * padded_count * width // cores,
            bytes_accessed=6 * features * width // cores,
            transcendentals=0,
        ),
        name="merge_own",
    )(kept_features, own, error_old, turned_q)
    merged_other, left_copies = pl.pallas_call(
        merge_other_kernel,
        out_shape=[
            jax.ShapeDtypeStruct((features, width // cores), F32),
            jax.ShapeDtypeStruct((across, rank, features), BF16),
        ],
        compiler_params=params(),
        name="merge_other",
    )(kept_features, other, error_old, turned_q, total)

    left_copies = add_copies(to_column(left_copies, 0), lax.axis_size("y"), BF16)
    left_copies = to_column(left_copies, 1)

    left, q_pieces = pl.pallas_call(
        functools.partial(project_kernel, replicas),
        out_shape=[
            jax.ShapeDtypeStruct((rank, features), F32),
            jax.ShapeDtypeStruct((crowd, rank + lines, lanes), F32),
        ],
        compiler_params=params(),
        name="project",
    )(left_copies, merged_own, merged_other)

    q_copies, gram = pl.pallas_call(
        functools.partial(add_blocks_kernel, rank),
        out_shape=[
            jax.ShapeDtypeStruct((across, rank, lanes), BF16),
            jax.ShapeDtypeStruct((lines, lanes), F32),
        ],
        compiler_params=params(),
        name="add_blocks",
    )(to_all(q_pieces, TENSOR))
    q_copies = add_copies(to_column(q_copies, 0), lax.axis_size("y"), F32)
    q_copies = add_copies(to_column(q_copies, 1), crowd, F32)
    q_pieces = to_all(q_copies, TENSOR)

    parts = features // LANES
    error_new, own_q = pl.pallas_call(
        functools.partial(finish_kernel, replicas),
        out_specs=[in_hbm(), whole((rank, lanes))],
        out_shape=[
            jax.ShapeDtypeStruct((features, width), BF16),
            jax.ShapeDtypeStruct((rank, lanes), F32),
        ],
        scratch_shapes=[
            pltpu.VMEM((rank, width), F32),
            pltpu.VMEM((4 * rank, width), BF16),
            pltpu.VMEM((parts, LANES, width), BF16),
            pltpu.SemaphoreType.DMA((parts,)),
        ],
        compiler_params=params(),
        name="finish",
    )(q_pieces, gram, left, merged_own, merged_other)
    return error_new, own_q.T


def solution(mesh, sizes=(8, 8, 4, 2)):
    finer = Mesh(mesh.devices.reshape(sizes), ("y", "z", "x", "c"))
    everyone = ("y", "z", "x", "c")
    in_specs = (P(DP, TENSOR), P(DP, TENSOR), P(everyone, None), P(), P())
    out_specs = (P(everyone, None), P(TENSOR, None))
    return jax.shard_map(
        body, mesh=finer, in_specs=in_specs, out_specs=out_specs, check_vma=False
    )
```

```python
import functools

import jax
import jax.numpy as jnp
from jax import lax
from jax.experimental import pallas as pl
from jax.experimental.pallas import tpu as pltpu
from jax.sharding import Mesh
from jax.sharding import PartitionSpec as P

DP = ("y", "z")
TENSOR = ("x", "c")
CHUNK = 256
LANES = 128
BLOCKS = 5
MIB = 1024 * 1024
F32 = jnp.float32
BF16 = jnp.bfloat16


def dot(a, b, contract, precision=None):
    return lax.dot_general(
        a, b, (contract, ((), ())), precision=precision, preferred_element_type=F32
    )


def params(limit=20 * MIB):
    return pltpu.CompilerParams(vmem_limit_bytes=limit)


def split(x):
    high = x.astype(BF16)
    return high, (x - high.astype(F32)).astype(BF16)


def kept_ranks(pauses, row_count):
    count = pauses.shape[0]
    row = lax.broadcasted_iota(jnp.int32, (count, count), 0)
    col = lax.broadcasted_iota(jnp.int32, (count, count), 1)
    wide = pauses.astype(F32).reshape(1, count)
    column = jnp.sum(jnp.where(row == col, wide, 0.0), axis=1, keepdims=True)
    spot = lax.broadcasted_iota(jnp.int32, (1, row_count), 1).astype(F32)
    before = jnp.sum(jnp.where(column < spot, 1.0, 0.0), axis=0, keepdims=True)
    struck = jnp.sum(jnp.where(column == spot, 1.0, 0.0), axis=0, keepdims=True)
    return jnp.where(struck > 0.0, -1.0, spot - before)


def kept_rows(ranks, values_ref, kept_count):
    row_count = values_ref.shape[0]
    size = kept_count // BLOCKS
    window = size + row_count - kept_count
    blocks = []
    for block in range(BLOCKS):
        start = block * size
        here = ranks if start == 0 else pltpu.roll(ranks, row_count - start, 1)
        rank = lax.broadcasted_iota(jnp.int32, (size, window), 0) + start
        pick = jnp.where(rank.astype(F32) == here[:, :window], 1.0, 0.0).astype(BF16)
        blocks.append(dot(pick, values_ref[start : start + window], ((1,), (0,))))
    return jnp.concatenate(blocks, axis=0)


def compact_cotangents_kernel(pause_hbm, cot_hbm, out_ref, pause_ref, cot_ref, sems):
    pauses = pltpu.make_async_copy(pause_hbm, pause_ref, sems.at[0])
    cots = pltpu.make_async_copy(cot_hbm, cot_ref, sems.at[1])
    pauses.start()
    cots.start()
    pauses.wait()
    ranks = kept_ranks(pause_ref[...], cot_ref.shape[0])
    cots.wait()
    kept = kept_rows(ranks, cot_ref, out_ref.shape[1]).astype(BF16)
    for copy in range(out_ref.shape[0]):
        out_ref[copy] = kept


def compact_features_kernel(kept_count, pause_ref, act_ref, out_ref):
    ranks = kept_ranks(pause_ref[...], act_ref.shape[0])
    kept = kept_rows(ranks, act_ref, kept_count)
    spare = jnp.zeros((out_ref.shape[1] - kept_count, kept.shape[1]), F32)
    out_ref[...] = jnp.concatenate([kept, spare], axis=0).T.astype(BF16)


def places(side, pieces, lanes):
    core = lax.axis_index("c")
    core = core if side == 0 else 1 - core
    return [pl.multiple_of((2 * piece + core) * lanes, lanes) for piece in range(pieces)]


def at_places(ref, starts, lanes):
    return jnp.concatenate([ref[:, pl.ds(start, lanes)] for start in starts], axis=1)


def merge_part(side, feat_ref, cot_ref, err_ref, q_ref, merged_ref):
    pieces, kept_count, lanes = cot_ref.shape
    rank = q_ref.shape[0]
    features, padded_count = feat_ref.shape
    wide = CHUNK // lanes
    starts = places(side, pieces, lanes)
    total = jnp.zeros((features, LANES), F32)
    for chunk in range(pieces // wide):
        group = range(chunk * wide, (chunk + 1) * wide)
        spots = [starts[piece] for piece in group]
        cots = jnp.concatenate([cot_ref[piece] for piece in group], axis=1)
        cots = jnp.concatenate([cots, jnp.zeros((padded_count - kept_count, CHUNK), BF16)], axis=0)
        old = at_places(err_ref, spots, lanes).astype(F32)
        merged = dot(feat_ref[...], cots, ((1,), (0,))) + old
        merged_ref[:, chunk * CHUNK : (chunk + 1) * CHUNK] = merged
        m_high, m_low = split(merged)
        high, low = split(at_places(q_ref, spots, lanes))
        upper = jnp.concatenate([high, high], axis=1)
        lower = jnp.concatenate([low, jnp.zeros_like(low)], axis=1)
        spare = jnp.zeros((LANES - 2 * rank, 2 * CHUNK), BF16)
        total += dot(
            jnp.concatenate([m_high, m_low], axis=1),
            jnp.concatenate([upper, lower, spare], axis=0),
            ((1,), (1,)),
        )
    return total


def merge_own_kernel(feat_ref, own_ref, err_ref, q_ref, merged_ref, total_ref):
    total_ref[...] = merge_part(0, feat_ref, own_ref, err_ref, q_ref, merged_ref)


def merge_other_kernel(feat_ref, other_ref, err_ref, q_ref, total_ref, merged_ref, left_ref):
    rank = q_ref.shape[0]
    total = total_ref[...] + merge_part(1, feat_ref, other_ref, err_ref, q_ref, merged_ref)
    turned = total.T
    left = (turned[:rank] + turned[rank : 2 * rank]).astype(BF16)
    for copy in range(left_ref.shape[0]):
        left_ref[copy] = left


def add_copies_kernel(in_ref, out_ref):
    total = in_ref[0].astype(F32)
    for copy in range(1, in_ref.shape[0]):
        total += in_ref[copy].astype(F32)
    total = total.astype(out_ref.dtype)
    for copy in range(out_ref.shape[0]):
        out_ref[copy] = total


def pack(gram, lines):
    rank = gram.shape[0]
    wide = jnp.concatenate([gram, jnp.zeros((rank, LANES - rank), F32)], axis=1)
    total = wide[:lines]
    for block in range(1, rank // lines):
        total += pltpu.roll(wide[block * lines : (block + 1) * lines], block * rank, 1)
    return total


def unpack(packed, rank):
    lines = packed.shape[0]
    blocks = [packed[:, :rank]]
    for block in range(1, rank // lines):
        blocks.append(pltpu.roll(packed, LANES - block * rank, 1)[:, :rank])
    return jnp.concatenate(blocks, axis=0)


def project_kernel(replicas, in_ref, own_ref, other_ref, left_ref, out_ref):
    rank = left_ref.shape[0]
    pieces, lines, lanes = out_ref.shape
    wide = CHUNK // lanes
    total = in_ref[0].astype(F32)
    for copy in range(1, in_ref.shape[0]):
        total += in_ref[copy].astype(F32)
    total = total / replicas
    left_ref[...] = total
    high, low = split(total)
    stack = jnp.concatenate([high, low], axis=0)
    gram = dot(total, total, ((1,), (1,)), lax.Precision.HIGHEST)
    packed = pack(gram, lines - rank)
    for side, merged_ref in enumerate((own_ref, other_ref)):
        core = lax.axis_index("c")
        core = core if side == 0 else 1 - core
        for chunk in range(merged_ref.shape[1] // CHUNK):
            m_high, m_low = split(merged_ref[:, chunk * CHUNK : (chunk + 1) * CHUNK])
            both = dot(stack, m_high, ((1,), (0,)))
            part = both[:rank] + both[rank:] + dot(high, m_low, ((1,), (0,)))
            for piece in range(wide):
                here = 2 * (chunk * wide + piece) + core
                out_ref[here, :rank] = part[:, piece * lanes : (piece + 1) * lanes]
                out_ref[here, rank:] = packed


def add_blocks_kernel(rank, in_ref, out_ref, gram_ref):
    total = in_ref[0]
    for copy in range(1, in_ref.shape[0]):
        total += in_ref[copy]
    for copy in range(out_ref.shape[0]):
        out_ref[copy] = total[:rank].astype(out_ref.dtype)
    gram_ref[...] = total[rank:]


def inverse_factor(gram):
    rank = gram.shape[0]
    row = lax.broadcasted_iota(jnp.int32, (rank, rank), 0)
    col = lax.broadcasted_iota(jnp.int32, (rank, rank), 1)
    spare = jnp.zeros((rank, LANES - 2 * rank), F32)
    table = jnp.concatenate([jnp.where(row == col, 1.0, 0.0), gram, spare], axis=1)
    line = lax.broadcasted_iota(jnp.int32, (rank, LANES), 0)
    pivots = jnp.ones((rank, LANES), F32)
    for k in range(0, rank, 2):
        at = rank + k
        column = jnp.broadcast_to(table[:, at : at + 1], (rank, LANES))
        second = jnp.broadcast_to(table[:, at + 1 : at + 2], (rank, LANES))
        pivot = column[k : k + 1]
        inverse = 1.0 / pivot
        slope = column[k + 1 : k + 2] * inverse
        after = second[k + 1 : k + 2] - slope * second[k : k + 1]
        top = table[k : k + 1]
        bottom = table[k + 1 : k + 2] - slope * top
        below = line > k + 1
        upper = jnp.where(below, column * inverse, 0.0)
        lower = jnp.where(below, second - slope * column, 0.0) * (1.0 / after)
        table = jnp.where(line == k + 1, bottom, table - upper * top - lower * bottom)
        pivots = jnp.where(line == k, pivot, jnp.where(line == k + 1, after, pivots))
    return (table / jnp.sqrt(pivots))[:, :rank]


def finish_kernel(
    replicas,
    in_ref,
    gram_ref,
    left_ref,
    own_merged_ref,
    other_merged_ref,
    err_hbm,
    own_ref,
    q_ref,
    stack_ref,
    err_ref,
    sems,
):
    rank, width = q_ref.shape
    inverse = inverse_factor(unpack(gram_ref[...], rank))
    raw = jnp.concatenate([in_ref[piece] for piece in range(in_ref.shape[0])], axis=1)
    raw = raw / replicas
    q_ref[...] = raw
    lanes = own_ref.shape[1]
    place = lax.axis_index("x") * lax.axis_size("c") + lax.axis_index("c")
    own = q_ref[:, pl.ds(pl.multiple_of(place * lanes, lanes), lanes)]
    own_ref[...] = dot(inverse, own, ((1,), (0,)), lax.Precision.HIGHEST)
    square = dot(inverse.T, inverse, ((1,), (0,)), lax.Precision.HIGHEST)
    high, low = split(dot(square, raw, ((1,), (0,)), lax.Precision.HIGHEST))
    stack_ref[...] = jnp.concatenate([high, high, low, jnp.zeros_like(high)], axis=0)
    high, low = split(left_ref[...])
    high = high.astype(F32)
    low = low.astype(F32)
    turned = jnp.concatenate([high, low, high, jnp.zeros_like(high)], axis=0).T.astype(BF16)
    sides = []
    for side, merged_ref in enumerate((own_merged_ref, other_merged_ref)):
        starts = places(side, merged_ref.shape[1] // lanes, lanes)
        sides.append((merged_ref, starts, at_places(stack_ref, starts, lanes)))
    stores = []
    chunks, rows, _ = err_ref.shape
    for chunk in range(chunks):
        here = slice(chunk * rows, (chunk + 1) * rows)
        for merged_ref, starts, stack in sides:
            fresh = merged_ref[here] - dot(turned[here], stack, ((1,), (0,)))
            for piece, start in enumerate(starts):
                block = fresh[:, piece * lanes : (piece + 1) * lanes].astype(BF16)
                err_ref[chunk, :, pl.ds(start, lanes)] = block
        stores.append(
            pltpu.make_async_copy(
                err_ref.at[chunk], err_hbm.at[pl.ds(chunk * rows, rows)], sems.at[chunk]
            )
        )
        stores[-1].start()
    for store in stores:
        store.wait()


def in_hbm():
    return pl.BlockSpec(memory_space=pltpu.HBM)


def kept_in_hbm(x):
    return pltpu.with_memory_space_constraint(x, pltpu.HBM)


def whole(shape):
    return pl.BlockSpec(shape, lambda *_: (0,) * len(shape))


def to_column(pieces, turn):
    axes = ("y", "z", "c")
    ny, nz, nc = (lax.axis_size(axis) for axis in axes)
    groups = []
    for core in range(nc):
        if (core + turn) % 2 == 0:
            groups += [[(y * nz + z) * nc + core for z in range(nz)] for y in range(ny)]
        else:
            groups += [[(y * nz + z) * nc + core for y in range(ny)] for z in range(nz)]
    return lax.all_to_all(
        pieces, axes, split_axis=0, concat_axis=0, tiled=True, axis_index_groups=groups
    )


def to_all(pieces, axes):
    return lax.all_to_all(pieces, axes, split_axis=0, concat_axis=0, tiled=True)


def add_copies(x, count, dtype):
    return pl.pallas_call(
        add_copies_kernel,
        out_shape=jax.ShapeDtypeStruct((count, *x.shape[1:]), dtype),
        compiler_params=params(),
        name="add_copies",
    )(x)


def body(activations, cotangents, error_old, pause_positions, initial_q):
    row_count, features = activations.shape
    lanes = cotangents.shape[1]
    width, rank = initial_q.shape
    kept_count = row_count - pause_positions.shape[0]
    padded_count = -(-kept_count // CHUNK) * CHUNK
    replicas = lax.axis_size(DP)
    line_x, across = lax.axis_size("x"), lax.axis_size("z")
    crowd = lax.axis_size(TENSOR)
    lines = rank * rank // LANES
    pauses = pause_positions

    cot_copies = pl.pallas_call(
        compact_cotangents_kernel,
        in_specs=[in_hbm(), in_hbm()],
        scratch_shapes=[
            pltpu.VMEM(pauses.shape, jnp.int32),
            pltpu.VMEM(cotangents.shape, BF16),
            pltpu.SemaphoreType.DMA((2,)),
        ],
        out_shape=jax.ShapeDtypeStruct((line_x, kept_count, lanes), BF16),
        compiler_params=params(),
        name="compact_cotangents",
    )(kept_in_hbm(pauses), kept_in_hbm(cotangents))
    own = to_all(cot_copies, "x")
    kept_features = pl.pallas_call(
        functools.partial(compact_features_kernel, kept_count),
        out_shape=jax.ShapeDtypeStruct((features, padded_count), BF16),
        compiler_params=params(),
        cost_estimate=pl.CostEstimate(
            flops=2 * kept_count * row_count * features,
            bytes_accessed=4 * row_count * features,
            transcendentals=0,
        ),
        name="compact_features",
    )(pauses, activations)
    cores = lax.axis_size("c")
    other = lax.ppermute(own, "c", [(i, cores - 1 - i) for i in range(cores)])

    turned_q = initial_q.T
    merged_own, total = pl.pallas_call(
        merge_own_kernel,
        out_shape=[
            jax.ShapeDtypeStruct((features, width // cores), F32),
            jax.ShapeDtypeStruct((features, LANES), F32),
        ],
        compiler_params=params(),
        cost_estimate=pl.CostEstimate(
            flops=2 * features * padded_count * width // cores,
            bytes_accessed=6 * features * width // cores,
            transcendentals=0,
        ),
        name="merge_own",
    )(kept_features, own, error_old, turned_q)
    merged_other, left_copies = pl.pallas_call(
        merge_other_kernel,
        out_shape=[
            jax.ShapeDtypeStruct((features, width // cores), F32),
            jax.ShapeDtypeStruct((across, rank, features), BF16),
        ],
        compiler_params=params(),
        name="merge_other",
    )(kept_features, other, error_old, turned_q, total)

    left_copies = add_copies(to_column(left_copies, 0), lax.axis_size("y"), BF16)
    left_copies = to_column(left_copies, 1)

    left, q_pieces = pl.pallas_call(
        functools.partial(project_kernel, replicas),
        out_shape=[
            jax.ShapeDtypeStruct((rank, features), F32),
            jax.ShapeDtypeStruct((crowd, rank + lines, lanes), F32),
        ],
        compiler_params=params(),
        name="project",
    )(left_copies, merged_own, merged_other)

    q_copies, gram = pl.pallas_call(
        functools.partial(add_blocks_kernel, rank),
        out_shape=[
            jax.ShapeDtypeStruct((across, rank, lanes), BF16),
            jax.ShapeDtypeStruct((lines, lanes), F32),
        ],
        compiler_params=params(),
        name="add_blocks",
    )(to_all(q_pieces, TENSOR))
    q_copies = add_copies(to_column(q_copies, 0), lax.axis_size("y"), F32)
    q_copies = add_copies(to_column(q_copies, 1), crowd, F32)
    q_pieces = to_all(q_copies, TENSOR)

    parts = features // LANES
    error_new, own_q = pl.pallas_call(
        functools.partial(finish_kernel, replicas),
        out_specs=[in_hbm(), whole((rank, lanes))],
        out_shape=[
            jax.ShapeDtypeStruct((features, width), BF16),
            jax.ShapeDtypeStruct((rank, lanes), F32),
        ],
        scratch_shapes=[
            pltpu.VMEM((rank, width), F32),
            pltpu.VMEM((4 * rank, width), BF16),
            pltpu.VMEM((parts, LANES, width), BF16),
            pltpu.SemaphoreType.DMA((parts,)),
        ],
        compiler_params=params(),
        name="finish",
    )(q_pieces, gram, left, merged_own, merged_other)
    return error_new, own_q.T


def solution(mesh, sizes=(8, 8, 4, 2)):
    finer = Mesh(mesh.devices.reshape(sizes), ("y", "z", "x", "c"))
    everyone = ("y", "z", "x", "c")
    in_specs = (P(DP, TENSOR), P(DP, TENSOR), P(everyone, None), P(), P())
    out_specs = (P(everyone, None), P(TENSOR, None))
    return jax.shard_map(
        body, mesh=finer, in_specs=in_specs, out_specs=out_specs, check_vma=False
    )
```

```python
import functools

import jax
import jax.numpy as jnp
from jax import lax
from jax.experimental import pallas as pl
from jax.experimental.pallas import tpu as pltpu
from jax.sharding import Mesh
from jax.sharding import PartitionSpec as P

DP = ("y", "z")
TENSOR = ("x", "c")
CHUNK = 256
LANES = 128
BLOCKS = 5
MIB = 1024 * 1024
F32 = jnp.float32
BF16 = jnp.bfloat16


def dot(a, b, contract, precision=None):
    return lax.dot_general(
        a, b, (contract, ((), ())), precision=precision, preferred_element_type=F32
    )


def params(limit=20 * MIB):
    return pltpu.CompilerParams(vmem_limit_bytes=limit)


def split(x):
    high = x.astype(BF16)
    return high, (x - high.astype(F32)).astype(BF16)


def kept_ranks(pauses, row_count):
    count = pauses.shape[0]
    row = lax.broadcasted_iota(jnp.int32, (count, count), 0)
    col = lax.broadcasted_iota(jnp.int32, (count, count), 1)
    wide = pauses.astype(F32).reshape(1, count)
    column = jnp.sum(jnp.where(row == col, wide, 0.0), axis=1, keepdims=True)
    spot = lax.broadcasted_iota(jnp.int32, (1, row_count), 1).astype(F32)
    before = jnp.sum(jnp.where(column < spot, 1.0, 0.0), axis=0, keepdims=True)
    struck = jnp.sum(jnp.where(column == spot, 1.0, 0.0), axis=0, keepdims=True)
    return jnp.where(struck > 0.0, -1.0, spot - before)


def kept_rows(ranks, values_ref, kept_count):
    row_count = values_ref.shape[0]
    size = kept_count // BLOCKS
    window = size + row_count - kept_count
    blocks = []
    for block in range(BLOCKS):
        start = block * size
        here = ranks if start == 0 else pltpu.roll(ranks, row_count - start, 1)
        rank = lax.broadcasted_iota(jnp.int32, (size, window), 0) + start
        pick = jnp.where(rank.astype(F32) == here[:, :window], 1.0, 0.0).astype(BF16)
        blocks.append(dot(pick, values_ref[start : start + window], ((1,), (0,))))
    return jnp.concatenate(blocks, axis=0)


def compact_cotangents_kernel(pause_hbm, cot_hbm, out_ref, ranks_ref, pause_ref, cot_ref, sems):
    pauses = pltpu.make_async_copy(pause_hbm, pause_ref, sems.at[0])
    cots = pltpu.make_async_copy(cot_hbm, cot_ref, sems.at[1])
    pauses.start()
    cots.start()
    pauses.wait()
    ranks = kept_ranks(pause_ref[...], cot_ref.shape[0])
    ranks_ref[...] = ranks
    cots.wait()
    kept = kept_rows(ranks, cot_ref, out_ref.shape[1]).astype(BF16)
    for copy in range(out_ref.shape[0]):
        out_ref[copy] = kept


def compact_features_kernel(kept_count, ranks_ref, act_ref, out_ref):
    kept = kept_rows(ranks_ref[...], act_ref, kept_count)
    spare = jnp.zeros((out_ref.shape[1] - kept_count, kept.shape[1]), F32)
    out_ref[...] = jnp.concatenate([kept, spare], axis=0).T.astype(BF16)


def places(side, pieces, lanes):
    core = lax.axis_index("c")
    core = core if side == 0 else 1 - core
    return [pl.multiple_of((2 * piece + core) * lanes, lanes) for piece in range(pieces)]


def at_places(ref, starts, lanes):
    return jnp.concatenate([ref[:, pl.ds(start, lanes)] for start in starts], axis=1)


def merge_part(side, feat_ref, cot_ref, err_ref, q_ref, merged_ref):
    pieces, kept_count, lanes = cot_ref.shape
    rank = q_ref.shape[0]
    features, padded_count = feat_ref.shape
    wide = CHUNK // lanes
    starts = places(side, pieces, lanes)
    total = jnp.zeros((features, LANES), F32)
    for chunk in range(pieces // wide):
        group = range(chunk * wide, (chunk + 1) * wide)
        spots = [starts[piece] for piece in group]
        cots = jnp.concatenate([cot_ref[piece] for piece in group], axis=1)
        cots = jnp.concatenate([cots, jnp.zeros((padded_count - kept_count, CHUNK), BF16)], axis=0)
        old = at_places(err_ref, spots, lanes).astype(F32)
        merged = dot(feat_ref[...], cots, ((1,), (0,))) + old
        merged_ref[:, chunk * CHUNK : (chunk + 1) * CHUNK] = merged
        m_high, m_low = split(merged)
        high, low = split(at_places(q_ref, spots, lanes))
        upper = jnp.concatenate([high, high], axis=1)
        lower = jnp.concatenate([low, jnp.zeros_like(low)], axis=1)
        spare = jnp.zeros((LANES - 2 * rank, 2 * CHUNK), BF16)
        total += dot(
            jnp.concatenate([m_high, m_low], axis=1),
            jnp.concatenate([upper, lower, spare], axis=0),
            ((1,), (1,)),
        )
    return total


def merge_own_kernel(feat_ref, own_ref, err_ref, q_ref, merged_ref, total_ref):
    total_ref[...] = merge_part(0, feat_ref, own_ref, err_ref, q_ref, merged_ref)


def merge_other_kernel(feat_ref, other_ref, err_ref, q_ref, total_ref, merged_ref, left_ref):
    rank = q_ref.shape[0]
    total = total_ref[...] + merge_part(1, feat_ref, other_ref, err_ref, q_ref, merged_ref)
    turned = total.T
    left = (turned[:rank] + turned[rank : 2 * rank]).astype(BF16)
    for copy in range(left_ref.shape[0]):
        left_ref[copy] = left


def add_copies_kernel(in_ref, out_ref):
    total = in_ref[0].astype(F32)
    for copy in range(1, in_ref.shape[0]):
        total += in_ref[copy].astype(F32)
    total = total.astype(out_ref.dtype)
    for copy in range(out_ref.shape[0]):
        out_ref[copy] = total


def pack(gram, lines):
    rank = gram.shape[0]
    wide = jnp.concatenate([gram, jnp.zeros((rank, LANES - rank), F32)], axis=1)
    total = wide[:lines]
    for block in range(1, rank // lines):
        total += pltpu.roll(wide[block * lines : (block + 1) * lines], block * rank, 1)
    return total


def unpack(packed, rank):
    lines = packed.shape[0]
    blocks = [packed[:, :rank]]
    for block in range(1, rank // lines):
        blocks.append(pltpu.roll(packed, LANES - block * rank, 1)[:, :rank])
    return jnp.concatenate(blocks, axis=0)


def project_kernel(replicas, in_ref, own_ref, other_ref, left_ref, out_ref):
    rank = left_ref.shape[0]
    pieces, lines, lanes = out_ref.shape
    wide = CHUNK // lanes
    total = in_ref[0].astype(F32)
    for copy in range(1, in_ref.shape[0]):
        total += in_ref[copy].astype(F32)
    total = total / replicas
    left_ref[...] = total
    high, low = split(total)
    stack = jnp.concatenate([high, low], axis=0)
    gram = dot(total, total, ((1,), (1,)), lax.Precision.HIGHEST)
    packed = pack(gram, lines - rank)
    for side, merged_ref in enumerate((own_ref, other_ref)):
        core = lax.axis_index("c")
        core = core if side == 0 else 1 - core
        for chunk in range(merged_ref.shape[1] // CHUNK):
            m_high, m_low = split(merged_ref[:, chunk * CHUNK : (chunk + 1) * CHUNK])
            both = dot(stack, m_high, ((1,), (0,)))
            part = both[:rank] + both[rank:] + dot(high, m_low, ((1,), (0,)))
            for piece in range(wide):
                here = 2 * (chunk * wide + piece) + core
                out_ref[here, :rank] = part[:, piece * lanes : (piece + 1) * lanes]
                out_ref[here, rank:] = packed


def add_blocks_kernel(rank, in_ref, out_ref, gram_ref):
    total = in_ref[0]
    for copy in range(1, in_ref.shape[0]):
        total += in_ref[copy]
    for copy in range(out_ref.shape[0]):
        out_ref[copy] = total[:rank].astype(out_ref.dtype)
    gram_ref[...] = total[rank:]


def inverse_factor(gram):
    rank = gram.shape[0]
    row = lax.broadcasted_iota(jnp.int32, (rank, rank), 0)
    col = lax.broadcasted_iota(jnp.int32, (rank, rank), 1)
    spare = jnp.zeros((rank, LANES - 2 * rank), F32)
    table = jnp.concatenate([jnp.where(row == col, 1.0, 0.0), gram, spare], axis=1)
    line = lax.broadcasted_iota(jnp.int32, (rank, LANES), 0)
    pivots = jnp.ones((rank, LANES), F32)
    for k in range(0, rank, 2):
        at = rank + k
        column = jnp.broadcast_to(table[:, at : at + 1], (rank, LANES))
        second = jnp.broadcast_to(table[:, at + 1 : at + 2], (rank, LANES))
        pivot = column[k : k + 1]
        inverse = 1.0 / pivot
        slope = column[k + 1 : k + 2] * inverse
        after = second[k + 1 : k + 2] - slope * second[k : k + 1]
        top = table[k : k + 1]
        bottom = table[k + 1 : k + 2] - slope * top
        below = line > k + 1
        upper = jnp.where(below, column * inverse, 0.0)
        lower = jnp.where(below, second - slope * column, 0.0) * (1.0 / after)
        table = jnp.where(line == k + 1, bottom, table - upper * top - lower * bottom)
        pivots = jnp.where(line == k, pivot, jnp.where(line == k + 1, after, pivots))
    return (table / jnp.sqrt(pivots))[:, :rank]


def finish_kernel(
    replicas,
    in_ref,
    gram_ref,
    left_ref,
    own_merged_ref,
    other_merged_ref,
    err_hbm,
    own_ref,
    q_ref,
    stack_ref,
    err_ref,
    sems,
):
    rank, width = q_ref.shape
    inverse = inverse_factor(unpack(gram_ref[...], rank))
    raw = jnp.concatenate([in_ref[piece] for piece in range(in_ref.shape[0])], axis=1)
    raw = raw / replicas
    q_ref[...] = raw
    lanes = own_ref.shape[1]
    place = lax.axis_index("x") * lax.axis_size("c") + lax.axis_index("c")
    own = q_ref[:, pl.ds(pl.multiple_of(place * lanes, lanes), lanes)]
    own_ref[...] = dot(inverse, own, ((1,), (0,)), lax.Precision.HIGHEST)
    square = dot(inverse.T, inverse, ((1,), (0,)), lax.Precision.HIGHEST)
    high, low = split(dot(square, raw, ((1,), (0,)), lax.Precision.HIGHEST))
    stack_ref[...] = jnp.concatenate([high, high, low, jnp.zeros_like(high)], axis=0)
    high, low = split(left_ref[...])
    high = high.astype(F32)
    low = low.astype(F32)
    turned = jnp.concatenate([high, low, high, jnp.zeros_like(high)], axis=0).T.astype(BF16)
    sides = []
    for side, merged_ref in enumerate((own_merged_ref, other_merged_ref)):
        starts = places(side, merged_ref.shape[1] // lanes, lanes)
        sides.append((merged_ref, starts, at_places(stack_ref, starts, lanes)))
    stores = []
    chunks, rows, _ = err_ref.shape
    for chunk in range(chunks):
        here = slice(chunk * rows, (chunk + 1) * rows)
        for merged_ref, starts, stack in sides:
            fresh = merged_ref[here] - dot(turned[here], stack, ((1,), (0,)))
            for piece, start in enumerate(starts):
                block = fresh[:, piece * lanes : (piece + 1) * lanes].astype(BF16)
                err_ref[chunk, :, pl.ds(start, lanes)] = block
        stores.append(
            pltpu.make_async_copy(
                err_ref.at[chunk], err_hbm.at[pl.ds(chunk * rows, rows)], sems.at[chunk]
            )
        )
        stores[-1].start()
    for store in stores:
        store.wait()


def in_hbm():
    return pl.BlockSpec(memory_space=pltpu.HBM)


def kept_in_hbm(x):
    return pltpu.with_memory_space_constraint(x, pltpu.HBM)


def whole(shape):
    return pl.BlockSpec(shape, lambda *_: (0,) * len(shape))


def to_column(pieces, turn):
    axes = ("y", "z", "c")
    ny, nz, nc = (lax.axis_size(axis) for axis in axes)
    groups = []
    for core in range(nc):
        if (core + turn) % 2 == 0:
            groups += [[(y * nz + z) * nc + core for z in range(nz)] for y in range(ny)]
        else:
            groups += [[(y * nz + z) * nc + core for y in range(ny)] for z in range(nz)]
    return lax.all_to_all(
        pieces, axes, split_axis=0, concat_axis=0, tiled=True, axis_index_groups=groups
    )


def to_all(pieces, axes):
    return lax.all_to_all(pieces, axes, split_axis=0, concat_axis=0, tiled=True)


def add_copies(x, count, dtype):
    return pl.pallas_call(
        add_copies_kernel,
        out_shape=jax.ShapeDtypeStruct((count, *x.shape[1:]), dtype),
        compiler_params=params(),
        name="add_copies",
    )(x)


def body(activations, cotangents, error_old, pause_positions, initial_q):
    row_count, features = activations.shape
    lanes = cotangents.shape[1]
    width, rank = initial_q.shape
    kept_count = row_count - pause_positions.shape[0]
    padded_count = -(-kept_count // CHUNK) * CHUNK
    replicas = lax.axis_size(DP)
    line_x, across = lax.axis_size("x"), lax.axis_size("z")
    crowd = lax.axis_size(TENSOR)
    lines = rank * rank // LANES
    pauses = pause_positions

    cot_copies, ranks = pl.pallas_call(
        compact_cotangents_kernel,
        in_specs=[in_hbm(), in_hbm()],
        scratch_shapes=[
            pltpu.VMEM(pauses.shape, jnp.int32),
            pltpu.VMEM(cotangents.shape, BF16),
            pltpu.SemaphoreType.DMA((2,)),
        ],
        out_shape=[
            jax.ShapeDtypeStruct((line_x, kept_count, lanes), BF16),
            jax.ShapeDtypeStruct((1, row_count), F32),
        ],
        compiler_params=params(),
        name="compact_cotangents",
    )(kept_in_hbm(pauses), kept_in_hbm(cotangents))
    own = to_all(cot_copies, "x")
    kept_features = pl.pallas_call(
        functools.partial(compact_features_kernel, kept_count),
        out_shape=jax.ShapeDtypeStruct((features, padded_count), BF16),
        compiler_params=params(),
        cost_estimate=pl.CostEstimate(
            flops=2 * kept_count * row_count * features,
            bytes_accessed=4 * row_count * features,
            transcendentals=0,
        ),
        name="compact_features",
    )(ranks, activations)
    cores = lax.axis_size("c")
    other = lax.ppermute(own, "c", [(i, cores - 1 - i) for i in range(cores)])

    turned_q = initial_q.T
    merged_own, total = pl.pallas_call(
        merge_own_kernel,
        out_shape=[
            jax.ShapeDtypeStruct((features, width // cores), F32),
            jax.ShapeDtypeStruct((features, LANES), F32),
        ],
        compiler_params=params(),
        cost_estimate=pl.CostEstimate(
            flops=2 * features * padded_count * width // cores,
            bytes_accessed=6 * features * width // cores,
            transcendentals=0,
        ),
        name="merge_own",
    )(kept_features, own, error_old, turned_q)
    merged_other, left_copies = pl.pallas_call(
        merge_other_kernel,
        out_shape=[
            jax.ShapeDtypeStruct((features, width // cores), F32),
            jax.ShapeDtypeStruct((across, rank, features), BF16),
        ],
        compiler_params=params(),
        name="merge_other",
    )(kept_features, other, error_old, turned_q, total)

    left_copies = add_copies(to_column(left_copies, 0), lax.axis_size("y"), BF16)
    left_copies = to_column(left_copies, 1)

    left, q_pieces = pl.pallas_call(
        functools.partial(project_kernel, replicas),
        out_shape=[
            jax.ShapeDtypeStruct((rank, features), F32),
            jax.ShapeDtypeStruct((crowd, rank + lines, lanes), F32),
        ],
        compiler_params=params(),
        name="project",
    )(left_copies, merged_own, merged_other)

    q_copies, gram = pl.pallas_call(
        functools.partial(add_blocks_kernel, rank),
        out_shape=[
            jax.ShapeDtypeStruct((across, rank, lanes), BF16),
            jax.ShapeDtypeStruct((lines, lanes), F32),
        ],
        compiler_params=params(),
        name="add_blocks",
    )(to_all(q_pieces, TENSOR))
    q_copies = add_copies(to_column(q_copies, 0), lax.axis_size("y"), F32)
    q_copies = add_copies(to_column(q_copies, 1), crowd, F32)
    q_pieces = to_all(q_copies, TENSOR)

    lines = LANES // 2
    parts = features // lines
    error_new, own_q = pl.pallas_call(
        functools.partial(finish_kernel, replicas),
        out_specs=[in_hbm(), whole((rank, lanes))],
        out_shape=[
            jax.ShapeDtypeStruct((features, width), BF16),
            jax.ShapeDtypeStruct((rank, lanes), F32),
        ],
        scratch_shapes=[
            pltpu.VMEM((rank, width), F32),
            pltpu.VMEM((4 * rank, width), BF16),
            pltpu.VMEM((parts, lines, width), BF16),
            pltpu.SemaphoreType.DMA((parts,)),
        ],
        compiler_params=params(),
        name="finish",
    )(q_pieces, gram, left, merged_own, merged_other)
    return error_new, own_q.T


def solution(mesh, sizes=(8, 8, 4, 2)):
    finer = Mesh(mesh.devices.reshape(sizes), ("y", "z", "x", "c"))
    everyone = ("y", "z", "x", "c")
    in_specs = (P(DP, TENSOR), P(DP, TENSOR), P(everyone, None), P(), P())
    out_specs = (P(everyone, None), P(TENSOR, None))
    return jax.shard_map(
        body, mesh=finer, in_specs=in_specs, out_specs=out_specs, check_vma=False
    )
```
